128 devices in a mesh: tile: 16 (over y, z), slab: 8 (over x, core).
Axes of the slice: x: 4, y: 4, z: 4, core: 2. Of those that a mesh axis runs over, the one named last changes fastest.
Arguments:
- volume: bfloat16 [16, 128, 64, 256], P('tile', 'slab'), may hold values from -24 to 24
- partner: int32 [16], replicated, may hold values from 0 to 15, as said below
- offsets: int32 [16], replicated, may hold values from 0 to 7
- starts: int32 [2048], P(('tile', 'slab')), may hold values from 0 to 192
- classifier: int32 [2048, 1], P(('tile', 'slab')), may hold values from 0 to 15; in each aligned block of 16 rows (0 to 15, 16 to 31, ...) at most 2 rows name the same one
- stem_weight: bfloat16 [16, 512, 256], P('tile'), may hold values from -0.25 to 0.25
- expand_weight: bfloat16 [16, 1, 256, 1024], P('tile'), may hold values from -0.375 to 0.375
- shrink_weight: bfloat16 [16, 1, 1024, 256], P('tile'), may hold values from -0.1875 to 0.1875
- head_weight: bfloat16 [16, 256, 8], P('tile'), may hold values from -0.375 to 0.375
Outputs:
- log_response: float32 [16, 128, 64, 256], P('tile', 'slab')
- logits: float32 [2048, 8], P(('tile', 'slab'))
The draws below stay inside these ranges and needn't reach their ends.
Inputs may be any that keep to these rules, and one draw needn't show every extreme that they name: partner[partner[t]] = t and partner[t] != t for every tile t. Among the 16 candidates of one device at most 2 name the same classifier.
All inputs are finite; a program needn't handle non-finite values.
Results may differ from the reference program's by a relative error of at most 0.0024.
Values may be sent and summed in bfloat16 or wider, within the bound.
No kernel may reach another device: no remote copies, remote signals or barrier semaphores. Data moves between devices by JAX's collectives and lax.ppermute only.
A program may use at most 320 MiB of HBM per device.

```python
import math
import jax
import jax.numpy as jnp
import numpy as np
from jax import lax

ZD = 16
YW = 64
XW = 256
OV = 32
OFFMAX = 8
CX = 64
CAND_DEV = 16
CAP = 2
C = 256
HID = 1024
NCLS = 8
BLOCKS = 1
PATCH = 512
TILES = 16
NZ = 128
CANDS = 2048
CLASSIFIERS = 16
N_TILE = 16
N_SLAB = 8


def draw_partner(key, part):
    half = TILES // 2
    first_key = jax.random.fold_in(key, 11)
    order_key = jax.random.fold_in(key, 12)
    anchor = jax.random.randint(first_key, (), 0, half).astype(jnp.int32)
    mate = anchor + half
    tile_ids = jnp.arange(TILES, dtype=jnp.int32)
    ranks = jax.random.permutation(order_key, tile_ids)
    ranks = jnp.where(tile_ids == anchor, -2, ranks)
    ranks = jnp.where(tile_ids == mate, -1, ranks)
    order = jnp.argsort(ranks, stable=True).astype(jnp.int32)
    paired = order.reshape(half, 2)
    matched = jnp.zeros((TILES,), jnp.int32)
    matched = matched.at[paired[:, 0]].set(paired[:, 1])
    matched = matched.at[paired[:, 1]].set(paired[:, 0])
    return matched


def with_ends(values, key, smallest, high):
    shape = values.shape
    spot = [jax.random.randint(jax.random.fold_in(key, axis), (), 0, shape[axis]) for axis in range(len(shape))]
    values = values.at[tuple(spot)].set(smallest)
    longest = shape.index(max(shape))
    spot[longest] = (spot[longest] + 1) % shape[longest]
    return values.at[tuple(spot)].set(high)


def block_scale(own_key, shape, pieces, smallest, top_value):
    factor_of, own = 1.0, jax.random.fold_in(own_key, 6)
    for position, blocks in pieces:
        heights = jnp.exp(jax.random.uniform(jax.random.fold_in(own, position), (blocks,), jnp.float32, smallest / len(pieces), top_value / len(pieces)))
        factor_of = factor_of * jnp.repeat(heights, shape[position] // blocks).reshape([-1 if axis == position else 1 for axis in range(len(shape))])
    return factor_of


def shared_out(key, own, number, rows, count, top, reach, lean):
    ranking = jax.random.permutation(key, count)
    packed, ordinary = load_shares(count, rows * top, reach, lean, True), load_shares(count, rows * top, reach, lean, False)
    places = jnp.arange(count)

    def named(sizes, turn):
        used = int((sizes > 0).sum())
        fixed = max(1, used // 4)
        shifted = fixed + (places - fixed + turn * (used - fixed)) % max(1, count - fixed)
        return jnp.zeros((count,), jnp.int32).at[ranking[jnp.where(places < fixed, places, shifted)]].set(jnp.asarray(sizes, jnp.int32))

    sizes = jnp.where(number % 4 == 0, named(packed, number // 4), named(ordinary, number - number // 4 - 1))
    mixed = jax.random.permutation(jax.random.fold_in(own, 3), count)
    source_of, sink = mixed[0:count // 2 * 2:2], mixed[1:count // 2 * 2:2]
    slack = jnp.minimum(sizes[source_of] - 1, reach - sizes[sink]) // 2
    slack = jnp.where((source_of == ranking[0]) | (sink == ranking[0]) | (sizes[sink] == 0), 0, jnp.maximum(slack, 0))
    shifted = jax.random.randint(jax.random.fold_in(own, 4), (count // 2,), 0, 1 << 20) % (slack + 1)
    sizes = sizes.at[source_of].add(-shifted).at[sink].add(shifted)
    labels = jnp.searchsorted(jnp.cumsum(sizes), jnp.arange(rows * top), side="right").astype(jnp.int32)
    grid = labels.reshape(top, rows).T
    grid = grid[jax.random.permutation(jax.random.fold_in(own, 1), rows)]
    turn = jax.random.randint(jax.random.fold_in(own, 2), (rows, 1), 0, top)
    return jnp.take_along_axis(grid, (jnp.arange(top)[None, :] + turn) % top, axis=1)


def load_shares(amount, total, reach, lean, full):
    loads = [(1 << 20) // math.isqrt(rank ** lean) + 1 for rank in range(1, amount + 1)]
    largest = reach if full else min(reach, max(-(-total // amount), total * loads[0] // sum(loads)))
    least = 1 if total - largest >= amount - 1 else 0
    counts, surplus = [largest] + [least] * (amount - 1), total - largest - least * (amount - 1)
    while surplus > 0:
        free = [i for i in range(1, amount) if counts[i] < largest] or [i for i in range(1, amount) if counts[i] < reach]
        mass, remaining = sum([loads[i] for i in free]), surplus
        for i in free:
            addition = min(reach - counts[i], max(1, remaining * loads[i] // mass), surplus)
            counts[i] = counts[i] + addition
            surplus = surplus - addition
    return np.array(counts)


def normal_values(rng, shape, spread, most, split=(), kind=jnp.bfloat16):
    result = jax.random.normal(rng, shape, jnp.float32) * spread
    if len(split) > 0:
        result = block_scale(rng, shape, split, -0.22, 0.18) * result
    return jnp.clip(result, min=-most, max=most).astype(kind)


def setup_inputs(seed: int = 0) -> dict:
    key_list = jax.random.split(jax.random.key(seed), 10)
    volume = normal_values(key_list[0], (TILES, NZ, YW, XW), 4.0, 24.0, ((0, 16), (1, 8)))
    partner = draw_partner(jax.random.fold_in(key_list[9], 71), 0)
    offsets = with_ends(jax.random.randint(key_list[2], (TILES,), 0, OFFMAX), jax.random.fold_in(key_list[2], 1), 0, OFFMAX - 1).astype(jnp.int32)
    starts = with_ends(jax.random.randint(key_list[3], (CANDS,), 0, XW - CX + 1), jax.random.fold_in(key_list[3], 1), 0, XW - CX).astype(jnp.int32)
    classifier_keys = jax.random.split(jax.random.fold_in(key_list[4], 1), CANDS // CAND_DEV)
    classifier_turns = jax.random.permutation(jax.random.fold_in(key_list[4], 3), CANDS // CAND_DEV)
    classifier = jax.vmap(lambda own, number: shared_out(jax.random.fold_in(key_list[4], 2), own, number, CAND_DEV, CLASSIFIERS, 1, CAP, 2))(classifier_keys, classifier_turns).reshape((CANDS, 1))
    stem_weight = normal_values(key_list[5], (CLASSIFIERS, PATCH, C), PATCH ** -0.5, 0.25, ((0, 16),))
    expand_weight = normal_values(key_list[6], (CLASSIFIERS, BLOCKS, C, HID), C ** -0.5, 0.375, ((0, 16),))
    shrink_weight = normal_values(key_list[7], (CLASSIFIERS, BLOCKS, HID, C), HID ** -0.5, 0.1875, ((0, 16),))
    head_weight = normal_values(key_list[8], (CLASSIFIERS, C, NCLS), C ** -0.5, 0.375, ((0, 16),))
    return dict(volume=volume, partner=partner, offsets=offsets, starts=starts, classifier=classifier, stem_weight=stem_weight, expand_weight=expand_weight, shrink_weight=shrink_weight, head_weight=head_weight)


RADIUS = 3

def gauss_taps():
    weights_raw = [math.exp(-0.5 * j * j) for j in range(-RADIUS, RADIUS + 1)]
    summed = sum(weights_raw)
    return [value / summed for value in weights_raw]

def taps_sum(padded, axis, length):
    coeffs = gauss_taps()
    running = coeffs[0] * lax.slice_in_dim(padded, 0, length, axis=axis)
    for offset_tap in range(1, 2 * RADIUS + 1):
        running = running + coeffs[offset_tap] * lax.slice_in_dim(padded, offset_tap, offset_tap + length, axis=axis)
    return running

def smooth_axis(values, axis):
    padding = [(0, 0)] * values.ndim
    padding[axis] = (RADIUS, RADIUS)
    return taps_sum(jnp.pad(values, padding), axis, values.shape[axis])

def laplace(values):
    padded = jnp.pad(values, ((0, 0), (1, 1), (1, 1), (1, 1)))
    beside = padded[:, 2:, 1:-1, 1:-1] + padded[:, :-2, 1:-1, 1:-1]
    beside = beside + padded[:, 1:-1, 2:, 1:-1] + padded[:, 1:-1, :-2, 1:-1]
    beside = beside + padded[:, 1:-1, 1:-1, 2:] + padded[:, 1:-1, 1:-1, :-2]
    return beside - 6.0 * values

def patchify(cube_block):
    chans, planes, height, across = cube_block.shape
    shaped = cube_block.reshape(chans, planes // 4, 4, height // 8, 8, across // 8, 8)
    shaped = shaped.transpose(1, 3, 5, 0, 2, 4, 6)
    return shaped.reshape(planes // 4 * (height // 8) * (across // 8), chans * 256)

def classify(patches, stems, expands, shrinks, heads):
    hidden = jnp.einsum('npf,nfk->npk', patches.astype(jnp.float32), stems.astype(jnp.float32)).astype(jnp.bfloat16)
    for block_id in range(BLOCKS):
        wide = hidden.astype(jnp.float32)
        normed = (wide * lax.rsqrt(lax.optimization_barrier(jnp.mean(wide * wide, axis=-1, keepdims=True)) + 1e-05)).astype(jnp.bfloat16)
        expanded = jax.nn.relu(jnp.einsum('npk,nkh->nph', normed.astype(jnp.float32), expands[:, block_id].astype(jnp.float32))).astype(jnp.bfloat16)
        hidden = (wide + jnp.einsum('nph,nhk->npk', expanded.astype(jnp.float32), shrinks[:, block_id].astype(jnp.float32))).astype(jnp.bfloat16)
    pooled = lax.optimization_barrier(jnp.mean(hidden.astype(jnp.float32), axis=1))
    return jnp.einsum('nk,nkc->nc', pooled, heads.astype(jnp.float32), precision=lax.Precision.HIGHEST)

def reference(volume, partner, offsets, starts, classifier, stem_weight, expand_weight, shrink_weight, head_weight):
    values = volume.astype(jnp.float32)
    mates = volume[partner][..., :OV].astype(jnp.float32)
    row_ids = (jnp.arange(YW, dtype=jnp.int32)[None, :] - offsets[:, None]) % YW
    mates = jnp.take_along_axis(mates, row_ids[:, None, :, None], axis=2)
    column = jnp.arange(OV, dtype=jnp.float32)
    ramp = 0.25 + 0.5 * (column + 0.5) / OV
    blended = ramp * values[..., :OV] + (1.0 - ramp) * mates
    joined = jnp.concatenate([blended, values[..., OV:]], axis=3)
    smooth = smooth_axis(smooth_axis(smooth_axis(joined, 1), 2), 3)
    log_response = laplace(smooth)
    channel_pair = jnp.stack([smooth.astype(jnp.bfloat16), log_response.astype(jnp.bfloat16)], axis=1)
    zero = jnp.zeros((), jnp.int32)

    def one_device(device):
        tile_id = (device // N_SLAB).astype(jnp.int32)
        slab_id = (device % N_SLAB).astype(jnp.int32)
        band = lax.dynamic_slice(channel_pair, (tile_id, zero, slab_id * ZD, zero, zero), (1, 2, ZD, YW, XW))[0]
        first = (device * CAND_DEV).astype(jnp.int32)
        own_starts = lax.dynamic_slice_in_dim(starts, first, CAND_DEV)
        own_routes = lax.dynamic_slice_in_dim(classifier[:, 0], first, CAND_DEV)

        def cut(begin):
            return patchify(lax.dynamic_slice(band, (zero, zero, zero, begin.astype(jnp.int32)), (2, ZD, YW, CX)))
        patches = jax.vmap(cut)(own_starts)
        return classify(patches, stem_weight[own_routes], expand_weight[own_routes], shrink_weight[own_routes], head_weight[own_routes])
    scores = lax.map(one_device, jnp.arange(N_TILE * N_SLAB, dtype=jnp.int32))
    return (log_response, scores.reshape(CANDS, NCLS))
```

```python
import functools
import math

import jax
import jax.numpy as jnp
from jax import lax
from jax.experimental import pallas as pl
from jax.experimental.pallas import tpu as pltpu
from jax.sharding import PartitionSpec as P

OV = 32
CX = 64
RADIUS = 3
HALO = 4
F32 = jnp.float32
BF16 = jnp.bfloat16
HIGH = lax.Precision.HIGHEST

STEM_ROWS, EXPAND_ROWS, SHRINK_ROWS, HEAD_ROWS = 128, 256, 256, 16
EXPAND_AT = STEM_ROWS
SHRINK_AT = EXPAND_AT + EXPAND_ROWS
HEAD_AT = SHRINK_AT + SHRINK_ROWS
PART_ROWS = HEAD_AT + HEAD_ROWS


def gauss_taps():
    weights_raw = [math.exp(-0.5 * j * j) for j in range(-RADIUS, RADIUS + 1)]
    summed = sum(weights_raw)
    return [value / summed for value in weights_raw]


def pack_kernel(part_ref, stem_ref, expand_ref, shrink_ref, head_ref, out_ref, wide_ref):
    for half in range(2):
        lanes = pl.ds(128 * half, 128)
        wide_ref[...] = stem_ref[:, lanes].astype(F32)
        out_ref[pl.ds(64 * half, 64), :] = wide_ref[pl.ds(part_ref[0], 64, stride=8), :].astype(BF16)
        out_ref[pl.ds(SHRINK_AT + 128 * half, 128), :] = shrink_ref[:, lanes]
    out_ref[pl.ds(EXPAND_AT, 256), :] = expand_ref[...]
    out_ref[pl.ds(HEAD_AT, 16), :] = jnp.concatenate(
        [head_ref[:, :128].astype(F32), head_ref[:, 128:].astype(F32)], axis=0
    ).astype(BF16)


def pack_part(part, stem, expand, shrink, head):
    return pl.pallas_call(
        pack_kernel,
        out_shape=jax.ShapeDtypeStruct((PART_ROWS, 128), BF16),
        grid_spec=pltpu.PrefetchScalarGridSpec(
            num_scalar_prefetch=1,
            grid=(1,),
            in_specs=[
                pl.BlockSpec((512, 256), lambda i, p: (0, 0)),
                pl.BlockSpec((256, 128), lambda i, p: (0, p[0])),
                pl.BlockSpec((128, 256), lambda i, p: (p[0], 0)),
                pl.BlockSpec((8, 256), lambda i, p: (0, 0)),
            ],
            out_specs=pl.BlockSpec((PART_ROWS, 128), lambda i, p: (0, 0)),
            scratch_shapes=[pltpu.VMEM((512, 128), F32)],
        ),
        cost_estimate=pl.CostEstimate(flops=0, bytes_accessed=1 << 20, transcendentals=0),
        name="pack_part",
    )(part, stem, expand, shrink, head)


def band_kernel(
    scalars_ref, before_ref, own_ref, after_ref, mate_ref, log_ref, table_ref,
    joined_ref, rows_ref, smooth_ref, columns_ref,
):
    taps = gauss_taps()
    planes, rows, width = own_ref.shape
    offset, slab, slabs = scalars_ref[1], scalars_ref[2], scalars_ref[3]
    total = planes + 2 * HALO
    group = total // 4

    lane = lax.broadcasted_iota(jnp.int32, (rows, 128), 1)
    ramp = 0.25 + 0.5 * (lane.astype(F32) + 0.5) / OV
    for i in range(group):
        strip = pltpu.roll(mate_ref[0, i].astype(F32), offset, 0)
        for quarter in range(4):
            z = quarter * group + i
            if z < HALO:
                raw = before_ref[z]
            elif z < HALO + planes:
                raw = own_ref[z - HALO]
            else:
                raw = after_ref[z - HALO - planes]
            raw = raw.astype(F32)
            mate = strip if quarter == 0 else pltpu.roll(strip, 128 - 32 * quarter, 1)
            first = raw[:, :128]
            joined_ref[z, :, :128] = jnp.where(
                lane < OV, ramp * first + (1.0 - ramp) * mate, first
            )
            joined_ref[z, :, 128:] = raw[:, 128:]

    source = lax.broadcasted_iota(jnp.int32, (width, width), 0)
    target = lax.broadcasted_iota(jnp.int32, (width, width), 1)

    def band_matrix(shift):
        out = jnp.zeros((width, width), F32)
        for j in range(-RADIUS, RADIUS + 1):
            out = jnp.where(source - target == shift + j, taps[j + RADIUS], out)
        return out

    along = band_matrix(0)
    beside = jnp.where(target < width - 1, band_matrix(1), 0.0)
    beside = beside + jnp.where(target > 0, band_matrix(-1), 0.0)

    margin = jnp.zeros((planes + 2, 8, width), F32)
    rows_ref[:, :8, :] = margin
    rows_ref[:, 8 + rows :, :] = margin
    smooth_ref[:, :8, :] = margin
    smooth_ref[:, 8 + rows :, :] = margin

    for p in range(planes + 2):
        mixed = taps[0] * joined_ref[p]
        for j in range(1, 2 * RADIUS + 1):
            mixed = mixed + taps[j] * joined_ref[p + j]
        rows_ref[p, pl.ds(8, rows), :] = mixed
        mixed = taps[0] * rows_ref[p, pl.ds(8 - RADIUS, rows), :]
        for j in range(1, 2 * RADIUS + 1):
            mixed = mixed + taps[j] * rows_ref[p, pl.ds(8 - RADIUS + j, rows), :]
        smooth = jnp.dot(mixed, along, precision=HIGH, preferred_element_type=F32)
        if p == 0:
            smooth = jnp.where(slab > 0, smooth, 0.0)
        elif p == planes + 1:
            smooth = jnp.where(slab < slabs - 1, smooth, 0.0)
        else:
            log_ref[p - 1] = jnp.dot(mixed, beside, precision=HIGH, preferred_element_type=F32)
        smooth_ref[p, pl.ds(8, rows), :] = smooth
    for z in range(planes):
        p = z + 1
        here = smooth_ref[p, pl.ds(8, rows), :]
        near = smooth_ref[p - 1, pl.ds(8, rows), :] + smooth_ref[p + 1, pl.ds(8, rows), :]
        near = near + (smooth_ref[p, pl.ds(7, rows), :] + smooth_ref[p, pl.ds(9, rows), :])
        log_ref[z] = near + log_ref[z] - 6.0 * here

    count = (planes // 4) * (rows // 8)
    for a in range(planes // 4):
        for b in range(rows // 8):
            pieces = [
                smooth_ref[4 * a + dz + 1, pl.ds(8 + 8 * b, 8), :] for dz in range(4)
            ] + [log_ref[4 * a + dz, pl.ds(8 * b, 8), :] for dz in range(4)]
            block = jnp.concatenate(pieces, axis=0)
            block = jnp.concatenate([block, pltpu.roll(block, width - 1, 1)], axis=0)
            columns_ref[pl.ds(a * (rows // 8) + b, width, stride=count), :] = block.T
    table_ref[...] = columns_ref[...].astype(BF16)


def filter_band(scalars, before, own, after, mates):
    planes, rows, width = own.shape
    count = (planes // 4) * (rows // 8)
    whole3 = lambda i, s: (0, 0, 0)
    return pl.pallas_call(
        band_kernel,
        out_shape=(
            jax.ShapeDtypeStruct((planes, rows, width), F32),
            jax.ShapeDtypeStruct((width * count, 128), BF16),
        ),
        grid_spec=pltpu.PrefetchScalarGridSpec(
            num_scalar_prefetch=1,
            grid=(1,),
            in_specs=[
                pl.BlockSpec((HALO, rows, width), whole3),
                pl.BlockSpec((planes, rows, width), whole3),
                pl.BlockSpec((HALO, rows, width), whole3),
                pl.BlockSpec((1,) + mates.shape[1:], lambda i, s: (s[0], 0, 0, 0)),
            ],
            out_specs=(
                pl.BlockSpec((planes, rows, width), whole3),
                pl.BlockSpec((width * count, 128), lambda i, s: (0, 0)),
            ),
            scratch_shapes=[
                pltpu.VMEM((planes + 2 * HALO, rows, width), F32),
                pltpu.VMEM((planes + 2, rows + 16, width), F32),
                pltpu.VMEM((planes + 2, rows + 16, width), F32),
                pltpu.VMEM((width * count, 128), F32),
            ],
        ),
        compiler_params=pltpu.CompilerParams(vmem_limit_bytes=40 << 20),
        cost_estimate=pl.CostEstimate(
            flops=2_000_000_000, bytes_accessed=6 << 20, transcendentals=0
        ),
        name="filter_band",
    )(scalars, before, own, after, mates)


def classify_kernel(starts_ref, route_ref, table_ref, weight_ref, out_ref, score_ref):
    i = pl.program_id(0)
    begin = starts_ref[i]

    def rows_of(part, at, count):
        return weight_ref[0, part, pl.ds(at, count), :]

    def joined_lanes(parts, at, count):
        halves = [
            jnp.concatenate([rows_of(p, at + h * count, count) for p in parts], axis=0)
            for h in range(2)
        ]
        return jnp.concatenate(halves, axis=1)

    hidden = None
    for half in range(2):
        patches = jnp.concatenate(
            [
                jnp.concatenate(
                    [table_ref[begin + 8 * c + 4 * half + 2 * j] for j in range(2)], axis=1
                )
                for c in range(8)
            ],
            axis=0,
        )
        stem = joined_lanes(range(4 * half, 4 * half + 4), 0, 64)
        term = jnp.dot(patches, stem, preferred_element_type=F32)
        hidden = term if hidden is None else hidden + term
    wide = hidden.astype(BF16).astype(F32)
    power = jnp.mean(wide * wide, axis=-1, keepdims=True)
    normed = (wide * lax.rsqrt(power + 1e-05)).astype(BF16)
    total = wide
    for pair in range(4):
        parts = (2 * pair, 2 * pair + 1)
        expand = jnp.concatenate([rows_of(p, EXPAND_AT, 256) for p in parts], axis=1)
        up = jnp.dot(normed, expand, preferred_element_type=F32)
        up = jnp.maximum(up, 0.0).astype(BF16)
        shrink = joined_lanes(parts, SHRINK_AT, 128)
        total = total + jnp.dot(up, shrink, preferred_element_type=F32)
    last = total.astype(BF16).astype(F32)
    pooled = jnp.sum(last, axis=0, keepdims=True) * (1.0 / last.shape[0])
    head = rows_of(0, HEAD_AT, 16).astype(F32)
    products = head[:8] * pooled[:, :128] + head[8:] * pooled[:, 128:]
    scores = jnp.sum(products, axis=1, keepdims=True)
    lane = lax.broadcasted_iota(jnp.int32, (8, 128), 1)
    score_ref[...] = jnp.where(lane == i, scores, score_ref[...])

    @pl.when(i == pl.num_programs(0) - 1)
    def _():
        out_ref[...] = score_ref[...].T[: out_ref.shape[0], :]


def classify(starts, routes, table, weights):
    count = starts.shape[0]
    parts = weights.shape[1]
    return pl.pallas_call(
        classify_kernel,
        out_shape=jax.ShapeDtypeStruct((count, 8), F32),
        grid_spec=pltpu.PrefetchScalarGridSpec(
            num_scalar_prefetch=2,
            grid=(count,),
            in_specs=[
                pl.BlockSpec(table.shape, lambda i, s, r: (0, 0, 0)),
                pl.BlockSpec((1, parts, PART_ROWS, 128), lambda i, s, r: (r[i], 0, 0, 0)),
            ],
            out_specs=pl.BlockSpec((count, 8), lambda i, s, r: (0, 0)),
            scratch_shapes=[pltpu.VMEM((8, 128), F32)],
        ),
        compiler_params=pltpu.CompilerParams(vmem_limit_bytes=40 << 20),
        cost_estimate=pl.CostEstimate(
            flops=5_500_000_000, bytes_accessed=24 << 20, transcendentals=4096
        ),
        name="classify",
    )(starts, routes, table, weights)


def body(
    volume, partner, offsets, starts, classifier, stem_weight, expand_weight, shrink_weight, head_weight
):
    tile_me, slab_me = lax.axis_index("tile"), lax.axis_index("slab")
    tiles, slabs = lax.axis_size("tile"), lax.axis_size("slab")
    own = volume[0]
    planes, rows, width = own.shape

    part = pack_part(
        jnp.reshape(slab_me, (1,)).astype(jnp.int32),
        stem_weight[0], expand_weight[0, 0], shrink_weight[0, 0], head_weight[0].T,
    )
    weights = lax.all_gather(part, ("tile", "slab"), axis=0, tiled=False)
    weights = weights.reshape(tiles, slabs, PART_ROWS, 128)

    up = [(i, i + 1) for i in range(slabs - 1)]
    down = [(j, i) for i, j in up]
    before = lax.ppermute(own[planes - HALO :], "slab", up)
    after = lax.ppermute(own[:HALO], "slab", down)

    group = (planes + 2 * HALO) // 4
    strip = jnp.concatenate([before[:, :, :OV], own[:, :, :OV], after[:, :, :OV]], axis=0)
    strip = jnp.concatenate([strip[q * group : (q + 1) * group] for q in range(4)], axis=2)
    sent = jnp.broadcast_to(strip[None], (tiles,) + strip.shape)
    mates = lax.all_to_all(sent, "tile", split_axis=0, concat_axis=0, tiled=True)

    scalars = jnp.stack([partner[tile_me], offsets[tile_me], slab_me, jnp.int32(slabs)])
    log_response, table = filter_band(scalars, before, own, after, mates)
    table = table.reshape(width, -1, 128)
    logits = classify(starts, classifier[:, 0], table, weights)
    return (log_response[None], logits)


def solution(mesh):
    return jax.shard_map(
        body,
        mesh=mesh,
        in_specs=(
            P("tile", "slab", None, None),
            P(),
            P(),
            P(("tile", "slab")),
            P(("tile", "slab"), None),
            P("tile", None, None),
            P("tile", None, None, None),
            P("tile", None, None, None),
            P("tile", None, None),
        ),
        out_specs=(P("tile", "slab", None, None), P(("tile", "slab"), None)),
        check_vma=False,
    )
```

```python
import functools
import math

import jax
import jax.numpy as jnp
from jax import lax
from jax.experimental import pallas as pl
from jax.experimental.pallas import tpu as pltpu
from jax.sharding import PartitionSpec as P

OV = 32
CX = 64
RADIUS = 3
TOGETHER = 4
HALO = 4
F32 = jnp.float32
BF16 = jnp.bfloat16
HIGH = lax.Precision.HIGHEST

STEM_ROWS, EXPAND_ROWS, SHRINK_ROWS, HEAD_ROWS = 128, 256, 256, 16
EXPAND_AT = STEM_ROWS
SHRINK_AT = EXPAND_AT + EXPAND_ROWS
HEAD_AT = SHRINK_AT + SHRINK_ROWS
PART_ROWS = HEAD_AT + HEAD_ROWS


def gauss_taps():
    weights_raw = [math.exp(-0.5 * j * j) for j in range(-RADIUS, RADIUS + 1)]
    summed = sum(weights_raw)
    return [value / summed for value in weights_raw]


def pack_kernel(part_ref, stem_ref, expand_ref, shrink_ref, head_ref, out_ref, wide_ref):
    for half in range(2):
        lanes = pl.ds(128 * half, 128)
        wide_ref[...] = stem_ref[:, lanes].astype(F32)
        out_ref[pl.ds(64 * half, 64), :] = wide_ref[pl.ds(part_ref[0], 64, stride=8), :].astype(BF16)
        out_ref[pl.ds(SHRINK_AT + 128 * half, 128), :] = shrink_ref[:, lanes]
    out_ref[pl.ds(EXPAND_AT, 256), :] = expand_ref[...]
    out_ref[pl.ds(HEAD_AT, 16), :] = jnp.concatenate(
        [head_ref[:, :128].astype(F32), head_ref[:, 128:].astype(F32)], axis=0
    ).astype(BF16)


def pack_part(part, stem, expand, shrink, head):
    return pl.pallas_call(
        pack_kernel,
        out_shape=jax.ShapeDtypeStruct((PART_ROWS, 128), BF16),
        grid_spec=pltpu.PrefetchScalarGridSpec(
            num_scalar_prefetch=1,
            grid=(1,),
            in_specs=[
                pl.BlockSpec((512, 256), lambda i, p: (0, 0)),
                pl.BlockSpec((256, 128), lambda i, p: (0, p[0])),
                pl.BlockSpec((128, 256), lambda i, p: (p[0], 0)),
                pl.BlockSpec((8, 256), lambda i, p: (0, 0)),
            ],
            out_specs=pl.BlockSpec((PART_ROWS, 128), lambda i, p: (0, 0)),
            scratch_shapes=[pltpu.VMEM((512, 128), F32)],
        ),
        cost_estimate=pl.CostEstimate(flops=0, bytes_accessed=1 << 20, transcendentals=0),
        name="pack_part",
    )(part, stem, expand, shrink, head)


def band_kernel(
    scalars_ref, before_ref, own_ref, after_ref, mate_ref, log_ref, table_ref,
    joined_ref, rows_ref, smooth_ref, columns_ref,
):
    taps = gauss_taps()
    planes, rows, width = own_ref.shape
    offset, slab, slabs = scalars_ref[1], scalars_ref[2], scalars_ref[3]
    total = planes + 2 * HALO
    group = total // 4

    lane = lax.broadcasted_iota(jnp.int32, (rows, 128), 1)
    ramp = 0.25 + 0.5 * (lane.astype(F32) + 0.5) / OV
    for i in range(group):
        strip = pltpu.roll(mate_ref[0, i].astype(F32), offset, 0)
        for quarter in range(4):
            z = quarter * group + i
            if z < HALO:
                raw = before_ref[z]
            elif z < HALO + planes:
                raw = own_ref[z - HALO]
            else:
                raw = after_ref[z - HALO - planes]
            raw = raw.astype(F32)
            mate = strip if quarter == 0 else pltpu.roll(strip, 128 - 32 * quarter, 1)
            first = raw[:, :128]
            joined_ref[z, :, :128] = jnp.where(
                lane < OV, ramp * first + (1.0 - ramp) * mate, first
            )
            joined_ref[z, :, 128:] = raw[:, 128:]

    source = lax.broadcasted_iota(jnp.int32, (width, width), 0)
    target = lax.broadcasted_iota(jnp.int32, (width, width), 1)

    def band_matrix(shift):
        out = jnp.zeros((width, width), F32)
        for j in range(-RADIUS, RADIUS + 1):
            out = jnp.where(source - target == shift + j, taps[j + RADIUS], out)
        return out

    along = band_matrix(0)
    beside = jnp.where(target < width - 1, band_matrix(1), 0.0)
    beside = beside + jnp.where(target > 0, band_matrix(-1), 0.0)

    margin = jnp.zeros((planes + 2, 8, width), F32)
    rows_ref[:, :8, :] = margin
    rows_ref[:, 8 + rows :, :] = margin
    smooth_ref[:, :8, :] = margin
    smooth_ref[:, 8 + rows :, :] = margin

    for p in range(planes + 2):
        mixed = taps[0] * joined_ref[p]
        for j in range(1, 2 * RADIUS + 1):
            mixed = mixed + taps[j] * joined_ref[p + j]
        rows_ref[p, pl.ds(8, rows), :] = mixed
        mixed = taps[0] * rows_ref[p, pl.ds(8 - RADIUS, rows), :]
        for j in range(1, 2 * RADIUS + 1):
            mixed = mixed + taps[j] * rows_ref[p, pl.ds(8 - RADIUS + j, rows), :]
        smooth = jnp.dot(mixed, along, precision=HIGH, preferred_element_type=F32)
        if p == 0:
            smooth = jnp.where(slab > 0, smooth, 0.0)
        elif p == planes + 1:
            smooth = jnp.where(slab < slabs - 1, smooth, 0.0)
        else:
            log_ref[p - 1] = jnp.dot(mixed, beside, precision=HIGH, preferred_element_type=F32)
        smooth_ref[p, pl.ds(8, rows), :] = smooth
    for z in range(planes):
        p = z + 1
        here = smooth_ref[p, pl.ds(8, rows), :]
        near = smooth_ref[p - 1, pl.ds(8, rows), :] + smooth_ref[p + 1, pl.ds(8, rows), :]
        near = near + (smooth_ref[p, pl.ds(7, rows), :] + smooth_ref[p, pl.ds(9, rows), :])
        log_ref[z] = near + log_ref[z] - 6.0 * here

    count = (planes // 4) * (rows // 8)
    for a in range(planes // 4):
        for b in range(rows // 8):
            pieces = [
                smooth_ref[4 * a + dz + 1, pl.ds(8 + 8 * b, 8), :] for dz in range(4)
            ] + [log_ref[4 * a + dz, pl.ds(8 * b, 8), :] for dz in range(4)]
            block = jnp.concatenate(pieces, axis=0)
            block = jnp.concatenate([block, pltpu.roll(block, width - 1, 1)], axis=0)
            columns_ref[pl.ds(a * (rows // 8) + b, width, stride=count), :] = block.T
    table_ref[...] = columns_ref[...].astype(BF16)


def filter_band(scalars, before, own, after, mates):
    planes, rows, width = own.shape
    count = (planes // 4) * (rows // 8)
    whole3 = lambda i, s: (0, 0, 0)
    return pl.pallas_call(
        band_kernel,
        out_shape=(
            jax.ShapeDtypeStruct((planes, rows, width), F32),
            jax.ShapeDtypeStruct((width * count, 128), BF16),
        ),
        grid_spec=pltpu.PrefetchScalarGridSpec(
            num_scalar_prefetch=1,
            grid=(1,),
            in_specs=[
                pl.BlockSpec((HALO, rows, width), whole3),
                pl.BlockSpec((planes, rows, width), whole3),
                pl.BlockSpec((HALO, rows, width), whole3),
                pl.BlockSpec((1,) + mates.shape[1:], lambda i, s: (s[0], 0, 0, 0)),
            ],
            out_specs=(
                pl.BlockSpec((planes, rows, width), whole3),
                pl.BlockSpec((width * count, 128), lambda i, s: (0, 0)),
            ),
            scratch_shapes=[
                pltpu.VMEM((planes + 2 * HALO, rows, width), F32),
                pltpu.VMEM((planes + 2, rows + 16, width), F32),
                pltpu.VMEM((planes + 2, rows + 16, width), F32),
                pltpu.VMEM((width * count, 128), F32),
            ],
        ),
        compiler_params=pltpu.CompilerParams(vmem_limit_bytes=40 << 20),
        cost_estimate=pl.CostEstimate(
            flops=2_000_000_000, bytes_accessed=6 << 20, transcendentals=0
        ),
        name="filter_band",
    )(scalars, before, own, after, mates)


def classify_kernel(starts_ref, route_ref, table_ref, weight_ref, out_ref, held_ref, sem):
    count = out_ref.shape[1]

    def fetch(i):
        return pltpu.make_async_copy(weight_ref.at[route_ref[i]], held_ref.at[i], sem.at[i])

    for i in range(count):
        fetch(i).start()
    each = range(TOGETHER)
    lane = lax.broadcasted_iota(jnp.int32, (8, count), 1)

    def group(g, kept):
        first = TOGETHER * g
        for k in each:
            fetch(first + k).wait()

        def rows_of(k, part, at, rows):
            return held_ref[first + k, part, pl.ds(at, rows), :]

        def joined_lanes(k, parts, at, rows):
            halves = [
                jnp.concatenate([rows_of(k, p, at + h * rows, rows) for p in parts], axis=0)
                for h in range(2)
            ]
            return jnp.concatenate(halves, axis=1)

        hidden = [None] * TOGETHER
        for half in range(2):
            for k in each:
                begin = starts_ref[first + k]
                patches = jnp.concatenate(
                    [
                        jnp.concatenate(
                            [table_ref[begin + 8 * c + 4 * half + 2 * j] for j in range(2)], axis=1
                        )
                        for c in range(8)
                    ],
                    axis=0,
                )
                stem = joined_lanes(k, range(4 * half, 4 * half + 4), 0, 64)
                term = jnp.dot(patches, stem, preferred_element_type=F32)
                hidden[k] = term if half == 0 else hidden[k] + term
        total = [hidden[k].astype(BF16).astype(F32) for k in each]
        normed = []
        for k in each:
            power = jnp.mean(total[k] * total[k], axis=-1, keepdims=True)
            normed.append((total[k] * lax.rsqrt(power + 1e-05)).astype(BF16))
        for pair in range(4):
            parts = (2 * pair, 2 * pair + 1)
            up = []
            for k in each:
                expand = jnp.concatenate([rows_of(k, p, EXPAND_AT, 256) for p in parts], axis=1)
                wide = jnp.dot(normed[k], expand, preferred_element_type=F32)
                up.append(jnp.maximum(wide, 0.0).astype(BF16))
            for k in each:
                shrink = joined_lanes(k, parts, SHRINK_AT, 128)
                total[k] = total[k] + jnp.dot(up[k], shrink, preferred_element_type=F32)
        for k in each:
            last = total[k].astype(BF16).astype(F32)
            pooled = jnp.sum(last, axis=0, keepdims=True) * (1.0 / last.shape[0])
            head = rows_of(k, 0, HEAD_AT, 16).astype(F32)
            products = head[:8] * pooled[:, :128] + head[8:] * pooled[:, 128:]
            scores = jnp.sum(products, axis=1, keepdims=True)
            kept = jnp.where(lane == first + k, scores, kept)
        return kept

    out_ref[...] = lax.fori_loop(0, count // TOGETHER, group, jnp.zeros((8, count), F32))


def classify(starts, routes, table, weights):
    count = starts.shape[0]
    scores = pl.pallas_call(
        classify_kernel,
        out_shape=jax.ShapeDtypeStruct((8, count), F32),
        in_specs=[
            pl.BlockSpec(memory_space=pltpu.SMEM),
            pl.BlockSpec(memory_space=pltpu.SMEM),
            pl.BlockSpec(memory_space=pltpu.VMEM),
            pl.BlockSpec(memory_space=pl.ANY),
        ],
        out_specs=pl.BlockSpec(memory_space=pltpu.VMEM),
        scratch_shapes=[
            pltpu.VMEM((count,) + weights.shape[1:], BF16),
            pltpu.SemaphoreType.DMA((count,)),
        ],
        compiler_params=pltpu.CompilerParams(vmem_limit_bytes=48 << 20),
        cost_estimate=pl.CostEstimate(
            flops=5_500_000_000, bytes_accessed=24 << 20, transcendentals=4096
        ),
        name="classify",
    )(starts, routes, table, weights)
    return scores.T


def body(
    volume, partner, offsets, starts, classifier, stem_weight, expand_weight, shrink_weight, head_weight
):
    lines, posts = lax.axis_size("line"), lax.axis_size("post")
    tiles, slabs = lines * posts, lax.axis_size("slab")
    line_me, post_me = lax.axis_index("line"), lax.axis_index("post")
    tile_me, slab_me = line_me * posts + post_me, lax.axis_index("slab")
    own = volume[0]
    planes, rows, width = own.shape

    part = pack_part(
        jnp.reshape(slab_me, (1,)).astype(jnp.int32),
        stem_weight[0], expand_weight[0, 0], shrink_weight[0, 0], head_weight[0].T,
    )
    weights = lax.all_gather(part, ("line", "post", "slab"), axis=0, tiled=False)
    weights = weights.reshape(tiles, slabs, PART_ROWS, 128)

    up = [(i, i + 1) for i in range(slabs - 1)]
    down = [(j, i) for i, j in up]
    before = lax.ppermute(own[planes - HALO :], "slab", up)
    after = lax.ppermute(own[:HALO], "slab", down)

    group = (planes + 2 * HALO) // 4
    strip = jnp.concatenate([before[:, :, :OV], own[:, :, :OV], after[:, :, :OV]], axis=0)
    strip = jnp.concatenate([strip[q * group : (q + 1) * group] for q in range(4)], axis=2)
    sent = jnp.broadcast_to(strip[None], (posts,) + strip.shape)
    met = lax.all_to_all(sent, "post", split_axis=0, concat_axis=0, tiled=True)
    wanted = [partner[line * posts + post_me] % posts for line in range(lines)]
    sent = jnp.stack([lax.dynamic_index_in_dim(met, w, 0, keepdims=False) for w in wanted])
    mates = lax.all_to_all(sent, "line", split_axis=0, concat_axis=0, tiled=True)

    scalars = jnp.stack(
        [partner[tile_me] // posts, offsets[tile_me], slab_me, jnp.int32(slabs)]
    )
    log_response, table = filter_band(scalars, before, own, after, mates)
    table = table.reshape(width, -1, 128)
    logits = classify(starts, classifier[:, 0], table, weights)
    return (log_response[None], logits)


def solution(mesh):
    tiles, slabs = mesh.devices.shape
    posts = 4 if tiles % 4 == 0 else 1
    split = jax.sharding.Mesh(
        mesh.devices.reshape(tiles // posts, posts, slabs), ("line", "post", "slab")
    )
    tile = ("line", "post")
    both = ("line", "post", "slab")
    return jax.shard_map(
        body,
        mesh=split,
        in_specs=(
            P(tile, "slab", None, None),
            P(),
            P(),
            P(both),
            P(both, None),
            P(tile, None, None),
            P(tile, None, None, None),
            P(tile, None, None, None),
            P(tile, None, None),
        ),
        out_specs=(P(tile, "slab", None, None), P(both, None)),
        check_vma=False,
    )
```

```python
import functools
import math

import jax
import jax.numpy as jnp
from jax import lax
from jax.experimental import pallas as pl
from jax.experimental.pallas import tpu as pltpu
from jax.sharding import PartitionSpec as P

OV = 32
CX = 64
RADIUS = 3
TOGETHER = 4
HALO = 4
F32 = jnp.float32
BF16 = jnp.bfloat16
HIGH = lax.Precision.HIGHEST

STEM_ROWS, EXPAND_ROWS, SHRINK_ROWS, HEAD_ROWS = 128, 256, 256, 16
EXPAND_AT = STEM_ROWS
SHRINK_AT = EXPAND_AT + EXPAND_ROWS
HEAD_AT = SHRINK_AT + SHRINK_ROWS
PART_ROWS = HEAD_AT + HEAD_ROWS


def gauss_taps():
    weights_raw = [math.exp(-0.5 * j * j) for j in range(-RADIUS, RADIUS + 1)]
    summed = sum(weights_raw)
    return [value / summed for value in weights_raw]


def pack_kernel(core_ref, stem_ref, expand_ref, shrink_ref, head_ref, *refs):
    out_refs, wide_ref = refs[:2], refs[2]
    head = jnp.concatenate(
        [head_ref[:, :128].astype(F32), head_ref[:, 128:].astype(F32)], axis=0
    ).astype(BF16)
    for half in range(2):
        lanes = pl.ds(128 * half, 128)
        wide_ref[...] = stem_ref[:, lanes].astype(F32)
        for local in range(4):
            out_ref, q = out_refs[local // 2], local % 2
            rows = pl.ds(4 * core_ref[0] + local, 64, stride=8)
            out_ref[q, pl.ds(64 * half, 64), :] = wide_ref[rows, :].astype(BF16)
            out_ref[q, pl.ds(SHRINK_AT + 128 * half, 128), :] = shrink_ref[
                pl.ds(128 * local, 128), lanes
            ]
    for local in range(4):
        out_ref, q = out_refs[local // 2], local % 2
        out_ref[q, pl.ds(EXPAND_AT, 256), :] = expand_ref[:, pl.ds(128 * local, 128)]
        out_ref[q, pl.ds(HEAD_AT, 16), :] = head


def pack_parts(core, stem, expand, shrink, head):
    whole = pl.BlockSpec((2, PART_ROWS, 128), lambda i, c: (0, 0, 0))
    return pl.pallas_call(
        pack_kernel,
        out_shape=(jax.ShapeDtypeStruct((2, PART_ROWS, 128), BF16),) * 2,
        grid_spec=pltpu.PrefetchScalarGridSpec(
            num_scalar_prefetch=1,
            grid=(1,),
            in_specs=[
                pl.BlockSpec((512, 256), lambda i, c: (0, 0)),
                pl.BlockSpec((256, 512), lambda i, c: (0, c[0])),
                pl.BlockSpec((512, 256), lambda i, c: (c[0], 0)),
                pl.BlockSpec((8, 256), lambda i, c: (0, 0)),
            ],
            out_specs=(whole, whole),
            scratch_shapes=[pltpu.VMEM((512, 128), F32)],
        ),
        cost_estimate=pl.CostEstimate(flops=0, bytes_accessed=2 << 20, transcendentals=0),
        name="pack_parts",
    )(core, stem, expand, shrink, head)


def band_kernel(
    scalars_ref, before_ref, own_ref, after_ref, mate_ref, log_ref, table_ref,
    joined_ref, rows_ref, smooth_ref, columns_ref,
):
    taps = gauss_taps()
    planes, rows, width = own_ref.shape
    offset, slab, slabs = scalars_ref[1], scalars_ref[2], scalars_ref[3]
    total = planes + 2 * HALO
    group = total // 4

    lane = lax.broadcasted_iota(jnp.int32, (rows, 128), 1)
    ramp = 0.25 + 0.5 * (lane.astype(F32) + 0.5) / OV
    for i in range(group):
        strip = pltpu.roll(mate_ref[0, i].astype(F32), offset, 0)
        for quarter in range(4):
            z = quarter * group + i
            if z < HALO:
                raw = before_ref[z]
            elif z < HALO + planes:
                raw = own_ref[z - HALO]
            else:
                raw = after_ref[z - HALO - planes]
            raw = raw.astype(F32)
            mate = strip if quarter == 0 else pltpu.roll(strip, 128 - 32 * quarter, 1)
            first = raw[:, :128]
            joined_ref[z, :, :128] = jnp.where(
                lane < OV, ramp * first + (1.0 - ramp) * mate, first
            )
            joined_ref[z, :, 128:] = raw[:, 128:]

    source = lax.broadcasted_iota(jnp.int32, (width, width), 0)
    target = lax.broadcasted_iota(jnp.int32, (width, width), 1)

    def band_matrix(shift):
        out = jnp.zeros((width, width), F32)
        for j in range(-RADIUS, RADIUS + 1):
            out = jnp.where(source - target == shift + j, taps[j + RADIUS], out)
        return out

    along = band_matrix(0)
    beside = jnp.where(target < width - 1, band_matrix(1), 0.0)
    beside = beside + jnp.where(target > 0, band_matrix(-1), 0.0)

    margin = jnp.zeros((planes + 2, 8, width), F32)
    rows_ref[:, :8, :] = margin
    rows_ref[:, 8 + rows :, :] = margin
    smooth_ref[:, :8, :] = margin
    smooth_ref[:, 8 + rows :, :] = margin

    for p in range(planes + 2):
        mixed = taps[0] * joined_ref[p]
        for j in range(1, 2 * RADIUS + 1):
            mixed = mixed + taps[j] * joined_ref[p + j]
        rows_ref[p, pl.ds(8, rows), :] = mixed
        mixed = taps[0] * rows_ref[p, pl.ds(8 - RADIUS, rows), :]
        for j in range(1, 2 * RADIUS + 1):
            mixed = mixed + taps[j] * rows_ref[p, pl.ds(8 - RADIUS + j, rows), :]
        smooth = jnp.dot(mixed, along, precision=HIGH, preferred_element_type=F32)
        if p == 0:
            smooth = jnp.where(slab > 0, smooth, 0.0)
        elif p == planes + 1:
            smooth = jnp.where(slab < slabs - 1, smooth, 0.0)
        else:
            log_ref[p - 1] = jnp.dot(mixed, beside, precision=HIGH, preferred_element_type=F32)
        smooth_ref[p, pl.ds(8, rows), :] = smooth
    for z in range(planes):
        p = z + 1
        here = smooth_ref[p, pl.ds(8, rows), :]
        near = smooth_ref[p - 1, pl.ds(8, rows), :] + smooth_ref[p + 1, pl.ds(8, rows), :]
        near = near + (smooth_ref[p, pl.ds(7, rows), :] + smooth_ref[p, pl.ds(9, rows), :])
        log_ref[z] = near + log_ref[z] - 6.0 * here

    count = (planes // 4) * (rows // 8)
    for a in range(planes // 4):
        for b in range(rows // 8):
            pieces = [
                smooth_ref[4 * a + dz + 1, pl.ds(8 + 8 * b, 8), :] for dz in range(4)
            ] + [log_ref[4 * a + dz, pl.ds(8 * b, 8), :] for dz in range(4)]
            block = jnp.concatenate(pieces, axis=0)
            block = jnp.concatenate([block, pltpu.roll(block, width - 1, 1)], axis=0)
            columns_ref[pl.ds(a * (rows // 8) + b, width, stride=count), :] = block.T
    table_ref[...] = columns_ref[...].astype(BF16)


def filter_band(scalars, before, own, after, mates):
    planes, rows, width = own.shape
    count = (planes // 4) * (rows // 8)
    whole3 = lambda i, s: (0, 0, 0)
    return pl.pallas_call(
        band_kernel,
        out_shape=(
            jax.ShapeDtypeStruct((planes, rows, width), F32),
            jax.ShapeDtypeStruct((width * count, 128), BF16),
        ),
        grid_spec=pltpu.PrefetchScalarGridSpec(
            num_scalar_prefetch=1,
            grid=(1,),
            in_specs=[
                pl.BlockSpec((HALO, rows, width), whole3),
                pl.BlockSpec((planes, rows, width), whole3),
                pl.BlockSpec((HALO, rows, width), whole3),
                pl.BlockSpec((1,) + mates.shape[1:], lambda i, s: (s[0], 0, 0, 0)),
            ],
            out_specs=(
                pl.BlockSpec((planes, rows, width), whole3),
                pl.BlockSpec((width * count, 128), lambda i, s: (0, 0)),
            ),
            scratch_shapes=[
                pltpu.VMEM((planes + 2 * HALO, rows, width), F32),
                pltpu.VMEM((planes + 2, rows + 16, width), F32),
                pltpu.VMEM((planes + 2, rows + 16, width), F32),
                pltpu.VMEM((width * count, 128), F32),
            ],
        ),
        compiler_params=pltpu.CompilerParams(vmem_limit_bytes=40 << 20),
        cost_estimate=pl.CostEstimate(
            flops=2_000_000_000, bytes_accessed=6 << 20, transcendentals=0
        ),
        name="filter_band",
    )(scalars, before, own, after, mates)


def classify_kernel(starts_ref, place_ref, table_ref, *refs):
    weight_refs, (out_ref, held_ref, sem) = refs[:16], refs[16:]
    count = out_ref.shape[1]
    core = place_ref[8, 0]

    def copy(source, k, i, piece):
        holder = core if piece < 2 else 1 - core
        parts = pl.ds(4 * holder + 2 * (piece % 2), 2)
        return pltpu.make_async_copy(
            weight_refs[4 * piece + source].at[k], held_ref.at[i, parts], sem.at[i, piece]
        )

    def start(i, carry):
        for piece in range(4):
            chosen, k = place_ref[2 * piece, i], place_ref[2 * piece + 1, i]
            for source in range(4):

                @pl.when(chosen == source)
                def _():
                    copy(source, k, i, piece).start()

        return carry

    lax.fori_loop(0, 2 * TOGETHER, start, 0)
    each = range(TOGETHER)
    lane = lax.broadcasted_iota(jnp.int32, (8, count), 1)

    def group(g, kept):
        first = TOGETHER * g

        @pl.when(first + 2 * TOGETHER < count)
        def _():
            lax.fori_loop(first + 2 * TOGETHER, first + 3 * TOGETHER, start, 0)

        for k in each:
            for piece in range(4):
                copy(0, 0, first + k, piece).wait()

        def rows_of(k, part, at, rows):
            return held_ref[first + k, part, pl.ds(at, rows), :]

        def joined_lanes(k, parts, at, rows):
            halves = [
                jnp.concatenate([rows_of(k, p, at + h * rows, rows) for p in parts], axis=0)
                for h in range(2)
            ]
            return jnp.concatenate(halves, axis=1)

        hidden = [None] * TOGETHER
        for half in range(2):
            for k in each:
                begin = starts_ref[first + k]
                patches = jnp.concatenate(
                    [
                        jnp.concatenate(
                            [table_ref[begin + 8 * c + 4 * half + 2 * j] for j in range(2)], axis=1
                        )
                        for c in range(8)
                    ],
                    axis=0,
                )
                stem = joined_lanes(k, range(4 * half, 4 * half + 4), 0, 64)
                term = jnp.dot(patches, stem, preferred_element_type=F32)
                hidden[k] = term if half == 0 else hidden[k] + term
        total = [hidden[k].astype(BF16).astype(F32) for k in each]
        normed = []
        for k in each:
            power = jnp.mean(total[k] * total[k], axis=-1, keepdims=True)
            normed.append((total[k] * lax.rsqrt(power + 1e-05)).astype(BF16))
        for pair in range(4):
            parts = (2 * pair, 2 * pair + 1)
            up = []
            for k in each:
                expand = jnp.concatenate([rows_of(k, p, EXPAND_AT, 256) for p in parts], axis=1)
                wide = jnp.dot(normed[k], expand, preferred_element_type=F32)
                up.append(jnp.maximum(wide, 0.0).astype(BF16))
            for k in each:
                shrink = joined_lanes(k, parts, SHRINK_AT, 128)
                total[k] = total[k] + jnp.dot(up[k], shrink, preferred_element_type=F32)
        for k in each:
            last = total[k].astype(BF16).astype(F32)
            pooled = jnp.sum(last, axis=0, keepdims=True) * (1.0 / last.shape[0])
            head = rows_of(k, 0, HEAD_AT, 16).astype(F32)
            products = head[:8] * pooled[:, :128] + head[8:] * pooled[:, 128:]
            scores = jnp.sum(products, axis=1, keepdims=True)
            kept = jnp.where(lane == first + k, scores, kept)
        return kept

    out_ref[...] = lax.fori_loop(0, count // TOGETHER, group, jnp.zeros((8, count), F32))


def classify(starts, place, table, weights):
    count = starts.shape[0]
    scores = pl.pallas_call(
        classify_kernel,
        out_shape=jax.ShapeDtypeStruct((8, count), F32),
        in_specs=[
            pl.BlockSpec(memory_space=pltpu.SMEM),
            pl.BlockSpec(memory_space=pltpu.SMEM),
            pl.BlockSpec(memory_space=pltpu.VMEM),
        ]
        + [pl.BlockSpec(memory_space=pl.ANY)] * len(weights),
        out_specs=pl.BlockSpec(memory_space=pltpu.VMEM),
        scratch_shapes=[
            pltpu.VMEM((count, 8, PART_ROWS, 128), BF16),
            pltpu.SemaphoreType.DMA((count, 4)),
        ],
        compiler_params=pltpu.CompilerParams(vmem_limit_bytes=48 << 20),
        cost_estimate=pl.CostEstimate(
            flops=5_500_000_000, bytes_accessed=24 << 20, transcendentals=4096
        ),
        name="classify",
    )(starts, place, table, *weights)
    return scores.T


def ring(value, axis):
    size = lax.axis_size(axis)
    pairs = []
    for i in range(size):
        pairs.append((2 * i, 2 * ((i + 1) % size)))
        pairs.append((2 * i + 1, 2 * ((i - 1) % size) + 1))
    return lax.ppermute(value, (axis, "core"), pairs)


def around(value, axis):
    values = [value]
    for _ in range(lax.axis_size(axis) - 1):
        values.append(ring(values[-1], axis))
    return values


def body(
    volume, partner, offsets, starts, classifier, stem_weight, expand_weight, shrink_weight, head_weight
):
    lines, posts = lax.axis_size("line"), lax.axis_size("post")
    line_me, post_me = lax.axis_index("line"), lax.axis_index("post")
    slab_axes = ("column", "core")
    slabs, slab_me = lax.axis_size(slab_axes), lax.axis_index(slab_axes)
    tile_me, core_me = line_me * posts + post_me, lax.axis_index("core")
    own = volume[0]
    planes, rows, width = own.shape

    first, second = pack_parts(
        jnp.reshape(core_me, (1,)).astype(jnp.int32),
        stem_weight[0], expand_weight[0, 0], shrink_weight[0, 0], head_weight[0].T,
    )
    stream_a = around(jnp.stack(around(first, "post")), "line")
    stream_b = around(jnp.stack(around(second, "line")), "post")
    swap = [(0, 1), (1, 0)]
    weights = stream_a + stream_b
    weights = weights + [lax.ppermute(value, "core", swap) for value in weights]

    up = [(i, i + 1) for i in range(slabs - 1)]
    down = [(j, i) for i, j in up]
    before = lax.ppermute(own[planes - HALO :], slab_axes, up)
    after = lax.ppermute(own[:HALO], slab_axes, down)

    group = (planes + 2 * HALO) // 4
    strip = jnp.concatenate([before[:, :, :OV], own[:, :, :OV], after[:, :, :OV]], axis=0)
    strip = jnp.concatenate([strip[q * group : (q + 1) * group] for q in range(4)], axis=2)
    sent = jnp.broadcast_to(strip[None], (posts,) + strip.shape)
    met = lax.all_to_all(sent, "post", split_axis=0, concat_axis=0, tiled=True)
    wanted = [partner[line * posts + post_me] % posts for line in range(lines)]
    sent = jnp.stack([lax.dynamic_index_in_dim(met, w, 0, keepdims=False) for w in wanted])
    mates = lax.all_to_all(sent, "line", split_axis=0, concat_axis=0, tiled=True)

    scalars = jnp.stack(
        [partner[tile_me] // posts, offsets[tile_me], slab_me, jnp.int32(slabs)]
    )
    log_response, table = filter_band(scalars, before, own, after, mates)
    table = table.reshape(width, -1, 128)

    routes = classifier[:, 0]
    turn = 1 - 2 * core_me
    by_line = (turn * (line_me - routes // posts)) % lines
    by_post = (turn * (post_me - routes % posts)) % posts
    other_line, other_post = (lines - by_line) % lines, (posts - by_post) % posts
    place = jnp.stack(
        [
            by_line, by_post, by_post, by_line,
            other_line, other_post, other_post, other_line,
            jnp.broadcast_to(core_me, routes.shape),
        ]
    ).astype(jnp.int32)
    logits = classify(starts, place, table, weights)
    return (log_response[None], logits)


def solution(mesh):
    tiles, slabs = mesh.devices.shape
    split = jax.sharding.Mesh(
        mesh.devices.reshape(4, tiles // 4, slabs // 2, 2), ("line", "post", "column", "core")
    )
    tile, slab = ("line", "post"), ("column", "core")
    both = tile + slab
    return jax.shard_map(
        body,
        mesh=split,
        in_specs=(
            P(tile, slab, None, None),
            P(),
            P(),
            P(both),
            P(both, None),
            P(tile, None, None),
            P(tile, None, None, None),
            P(tile, None, None, None),
            P(tile, None, None),
        ),
        out_specs=(P(tile, slab, None, None), P(both, None)),
        check_vma=False,
    )
```

```python
import functools
import math

import jax
import jax.numpy as jnp
from jax import lax
from jax.experimental import pallas as pl
from jax.experimental.pallas import tpu as pltpu
from jax.sharding import PartitionSpec as P

OV = 32
CX = 64
RADIUS = 3
TOGETHER = 4
HALO = 4
F32 = jnp.float32
BF16 = jnp.bfloat16
HIGH = lax.Precision.HIGHEST

STEM_ROWS, EXPAND_ROWS, SHRINK_ROWS, HEAD_ROWS = 128, 256, 256, 16
EXPAND_AT = STEM_ROWS
SHRINK_AT = EXPAND_AT + EXPAND_ROWS
HEAD_AT = SHRINK_AT + SHRINK_ROWS
PART_ROWS = HEAD_AT + HEAD_ROWS
STRIP_ROWS = 128


def gauss_taps():
    weights_raw = [math.exp(-0.5 * j * j) for j in range(-RADIUS, RADIUS + 1)]
    summed = sum(weights_raw)
    return [value / summed for value in weights_raw]


def pack_kernel(core_ref, stem_ref, expand_ref, shrink_ref, head_ref, own_ref, *refs):
    out_refs, wide_ref = refs[:2], refs[2]
    head = jnp.concatenate(
        [head_ref[:, :128].astype(F32), head_ref[:, 128:].astype(F32)], axis=0
    ).astype(BF16)
    for half in range(2):
        lanes = pl.ds(128 * half, 128)
        wide_ref[...] = stem_ref[:, lanes].astype(F32)
        for local in range(4):
            out_ref, q = out_refs[local // 2], local % 2
            rows = pl.ds(4 * core_ref[0] + local, 64, stride=8)
            out_ref[q, pl.ds(64 * half, 64), :] = wide_ref[rows, :].astype(BF16)
            out_ref[q, pl.ds(SHRINK_AT + 128 * half, 128), :] = shrink_ref[
                pl.ds(128 * local, 128), lanes
            ]
    for local in range(4):
        out_ref, q = out_refs[local // 2], local % 2
        out_ref[q, pl.ds(EXPAND_AT, 256), :] = expand_ref[:, pl.ds(128 * local, 128)]
        out_ref[q, pl.ds(HEAD_AT, 16), :] = head
    planes, rows = own_ref.shape[0], own_ref.shape[1]
    lane = lax.broadcasted_iota(jnp.int32, (rows, 128), 1)
    for i in range(HALO):
        strip = own_ref[i].astype(F32)
        for quarter in range(1, planes // HALO):
            plane = pltpu.roll(own_ref[HALO * quarter + i].astype(F32), OV * quarter, 1)
            strip = jnp.where(lane >= OV * quarter, plane, strip)
        at = PART_ROWS + rows * (i % 2)
        out_refs[0][i // 2, pl.ds(at, rows), :] = strip.astype(BF16)


def pack_parts(core, stem, expand, shrink, head, own):
    wide = pl.BlockSpec((2, PART_ROWS + STRIP_ROWS, 128), lambda i, c: (0, 0, 0))
    whole = pl.BlockSpec((2, PART_ROWS, 128), lambda i, c: (0, 0, 0))
    return pl.pallas_call(
        pack_kernel,
        out_shape=(
            jax.ShapeDtypeStruct((2, PART_ROWS + STRIP_ROWS, 128), BF16),
            jax.ShapeDtypeStruct((2, PART_ROWS, 128), BF16),
        ),
        grid_spec=pltpu.PrefetchScalarGridSpec(
            num_scalar_prefetch=1,
            grid=(1,),
            in_specs=[
                pl.BlockSpec((512, 256), lambda i, c: (0, 0)),
                pl.BlockSpec((256, 512), lambda i, c: (0, c[0])),
                pl.BlockSpec((512, 256), lambda i, c: (c[0], 0)),
                pl.BlockSpec((8, 256), lambda i, c: (0, 0)),
                pl.BlockSpec(own.shape[:2] + (128,), lambda i, c: (0, 0, 0)),
            ],
            out_specs=(wide, whole),
            scratch_shapes=[pltpu.VMEM((512, 128), F32)],
        ),
        cost_estimate=pl.CostEstimate(flops=0, bytes_accessed=2 << 20, transcendentals=0),
        name="pack_parts",
    )(core, stem, expand, shrink, head, own)


def band_kernel(
    scalars_ref, before_ref, own_ref, after_ref, mate_before_ref, mate_ref, mate_after_ref,
    log_ref, table_ref, joined_ref, rows_ref, smooth_ref, columns_ref,
):
    taps = gauss_taps()
    planes, rows, width = own_ref.shape
    offset, slab, slabs = scalars_ref[0], scalars_ref[1], scalars_ref[2]

    lane = lax.broadcasted_iota(jnp.int32, (rows, 128), 1)
    ramp = 0.25 + 0.5 * (lane.astype(F32) + 0.5) / OV
    quarters = planes // HALO

    def stitch(z, raw, strip, quarter):
        raw = raw.astype(F32)
        mate = strip if quarter == 0 else pltpu.roll(strip, 128 - OV * quarter, 1)
        first = raw[:, :128]
        joined_ref[z, :, :128] = jnp.where(lane < OV, ramp * first + (1.0 - ramp) * mate, first)
        joined_ref[z, :, 128:] = raw[:, 128:]

    def turned(ref, i):
        return pltpu.roll(ref[i].astype(F32), offset, 0)

    for i in range(HALO):
        stitch(i, before_ref[i], turned(mate_before_ref, i), quarters - 1)
        stitch(HALO + planes + i, after_ref[i], turned(mate_after_ref, i), 0)
        strip = turned(mate_ref, i)
        for quarter in range(quarters):
            z = HALO * quarter + i
            stitch(HALO + z, own_ref[z], strip, quarter)

    source = lax.broadcasted_iota(jnp.int32, (width, width), 0)
    target = lax.broadcasted_iota(jnp.int32, (width, width), 1)

    def band_matrix(shift):
        out = jnp.zeros((width, width), F32)
        for j in range(-RADIUS, RADIUS + 1):
            out = jnp.where(source - target == shift + j, taps[j + RADIUS], out)
        return out

    along = band_matrix(0)
    beside = jnp.where(target < width - 1, band_matrix(1), 0.0)
    beside = beside + jnp.where(target > 0, band_matrix(-1), 0.0)

    margin = jnp.zeros((planes + 2, 8, width), F32)
    rows_ref[:, :8, :] = margin
    rows_ref[:, 8 + rows :, :] = margin
    smooth_ref[:, :8, :] = margin
    smooth_ref[:, 8 + rows :, :] = margin

    for p in range(planes + 2):
        mixed = taps[0] * joined_ref[p]
        for j in range(1, 2 * RADIUS + 1):
            mixed = mixed + taps[j] * joined_ref[p + j]
        rows_ref[p, pl.ds(8, rows), :] = mixed
        mixed = taps[0] * rows_ref[p, pl.ds(8 - RADIUS, rows), :]
        for j in range(1, 2 * RADIUS + 1):
            mixed = mixed + taps[j] * rows_ref[p, pl.ds(8 - RADIUS + j, rows), :]
        smooth = jnp.dot(mixed, along, precision=HIGH, preferred_element_type=F32)
        if p == 0:
            smooth = jnp.where(slab > 0, smooth, 0.0)
        elif p == planes + 1:
            smooth = jnp.where(slab < slabs - 1, smooth, 0.0)
        else:
            log_ref[p - 1] = jnp.dot(mixed, beside, precision=HIGH, preferred_element_type=F32)
        smooth_ref[p, pl.ds(8, rows), :] = smooth
    for z in range(planes):
        p = z + 1
        here = smooth_ref[p, pl.ds(8, rows), :]
        near = smooth_ref[p - 1, pl.ds(8, rows), :] + smooth_ref[p + 1, pl.ds(8, rows), :]
        near = near + (smooth_ref[p, pl.ds(7, rows), :] + smooth_ref[p, pl.ds(9, rows), :])
        log_ref[z] = near + log_ref[z] - 6.0 * here

    count = (planes // 4) * (rows // 8)
    for a in range(planes // 4):
        for b in range(rows // 8):
            pieces = [
                smooth_ref[4 * a + dz + 1, pl.ds(8 + 8 * b, 8), :] for dz in range(4)
            ] + [log_ref[4 * a + dz, pl.ds(8 * b, 8), :] for dz in range(4)]
            block = jnp.concatenate(pieces, axis=0)
            block = jnp.concatenate([block, pltpu.roll(block, width - 1, 1)], axis=0)
            columns_ref[pl.ds(a * (rows // 8) + b, width, stride=count), :] = block.T
    table_ref[...] = columns_ref[...].astype(BF16)


def filter_band(scalars, before, own, after, mate_before, mate, mate_after):
    planes, rows, width = own.shape
    count = (planes // 4) * (rows // 8)
    whole3 = lambda i, s: (0, 0, 0)
    return pl.pallas_call(
        band_kernel,
        out_shape=(
            jax.ShapeDtypeStruct((planes, rows, width), F32),
            jax.ShapeDtypeStruct((width * count, 128), BF16),
        ),
        grid_spec=pltpu.PrefetchScalarGridSpec(
            num_scalar_prefetch=1,
            grid=(1,),
            in_specs=[
                pl.BlockSpec((HALO, rows, width), whole3),
                pl.BlockSpec((planes, rows, width), whole3),
                pl.BlockSpec((HALO, rows, width), whole3),
            ]
            + [pl.BlockSpec(mate.shape, whole3)] * 3,
            out_specs=(
                pl.BlockSpec((planes, rows, width), whole3),
                pl.BlockSpec((width * count, 128), lambda i, s: (0, 0)),
            ),
            scratch_shapes=[
                pltpu.VMEM((planes + 2 * HALO, rows, width), F32),
                pltpu.VMEM((planes + 2, rows + 16, width), F32),
                pltpu.VMEM((planes + 2, rows + 16, width), F32),
                pltpu.VMEM((width * count, 128), F32),
            ],
        ),
        compiler_params=pltpu.CompilerParams(vmem_limit_bytes=40 << 20),
        cost_estimate=pl.CostEstimate(
            flops=2_000_000_000, bytes_accessed=6 << 20, transcendentals=0
        ),
        name="filter_band",
    )(scalars, before, own, after, mate_before, mate, mate_after)


def classify_kernel(starts_ref, place_ref, table_ref, *refs):
    weight_refs, (out_ref, held_ref, sem) = refs[:16], refs[16:]
    count = out_ref.shape[1]
    core = place_ref[8, 0]

    def copy(source, k, i, piece):
        holder = core if piece < 2 else 1 - core
        parts = pl.ds(4 * holder + 2 * (piece % 2), 2)
        return pltpu.make_async_copy(
            weight_refs[4 * piece + source].at[k], held_ref.at[i, parts], sem.at[i, piece]
        )

    def start(i, carry):
        for piece in range(4):
            chosen, k = place_ref[2 * piece, i], place_ref[2 * piece + 1, i]
            for source in range(4):

                @pl.when(chosen == source)
                def _():
                    copy(source, k, i, piece).start()

        return carry

    lax.fori_loop(0, 2 * TOGETHER, start, 0)
    each = range(TOGETHER)
    lane = lax.broadcasted_iota(jnp.int32, (8, count), 1)

    def group(g, kept):
        first = TOGETHER * g

        @pl.when(first + 2 * TOGETHER < count)
        def _():
            lax.fori_loop(first + 2 * TOGETHER, first + 3 * TOGETHER, start, 0)

        for k in each:
            for piece in range(4):
                copy(0, 0, first + k, piece).wait()

        def rows_of(k, part, at, rows):
            return held_ref[first + k, part, pl.ds(at, rows), :]

        def joined_lanes(k, parts, at, rows):
            halves = [
                jnp.concatenate([rows_of(k, p, at + h * rows, rows) for p in parts], axis=0)
                for h in range(2)
            ]
            return jnp.concatenate(halves, axis=1)

        hidden = [None] * TOGETHER
        for half in range(2):
            for k in each:
                begin = starts_ref[first + k]
                patches = jnp.concatenate(
                    [
                        jnp.concatenate(
                            [table_ref[begin + 8 * c + 4 * half + 2 * j] for j in range(2)], axis=1
                        )
                        for c in range(8)
                    ],
                    axis=0,
                )
                stem = joined_lanes(k, range(4 * half, 4 * half + 4), 0, 64)
                term = jnp.dot(patches, stem, preferred_element_type=F32)
                hidden[k] = term if half == 0 else hidden[k] + term
        total = [hidden[k].astype(BF16).astype(F32) for k in each]
        normed = []
        for k in each:
            power = jnp.mean(total[k] * total[k], axis=-1, keepdims=True)
            normed.append((total[k] * lax.rsqrt(power + 1e-05)).astype(BF16))
        for pair in range(4):
            parts = (2 * pair, 2 * pair + 1)
            up = []
            for k in each:
                expand = jnp.concatenate([rows_of(k, p, EXPAND_AT, 256) for p in parts], axis=1)
                wide = jnp.dot(normed[k], expand, preferred_element_type=F32)
                up.append(jnp.maximum(wide, 0.0).astype(BF16))
            for k in each:
                shrink = joined_lanes(k, parts, SHRINK_AT, 128)
                total[k] = total[k] + jnp.dot(up[k], shrink, preferred_element_type=F32)
        for k in each:
            last = total[k].astype(BF16).astype(F32)
            pooled = jnp.sum(last, axis=0, keepdims=True) * (1.0 / last.shape[0])
            head = rows_of(k, 0, HEAD_AT, 16).astype(F32)
            products = head[:8] * pooled[:, :128] + head[8:] * pooled[:, 128:]
            scores = jnp.sum(products, axis=1, keepdims=True)
            kept = jnp.where(lane == first + k, scores, kept)
        return kept

    out_ref[...] = lax.fori_loop(0, count // TOGETHER, group, jnp.zeros((8, count), F32))


def classify(starts, place, table, weights):
    count = starts.shape[0]
    scores = pl.pallas_call(
        classify_kernel,
        out_shape=jax.ShapeDtypeStruct((8, count), F32),
        in_specs=[
            pl.BlockSpec(memory_space=pltpu.SMEM),
            pl.BlockSpec(memory_space=pltpu.SMEM),
            pl.BlockSpec(memory_space=pltpu.VMEM),
        ]
        + [pl.BlockSpec(memory_space=pl.ANY)] * len(weights),
        out_specs=pl.BlockSpec(memory_space=pltpu.VMEM),
        scratch_shapes=[
            pltpu.VMEM((count, 8, PART_ROWS, 128), BF16),
            pltpu.SemaphoreType.DMA((count, 4)),
        ],
        compiler_params=pltpu.CompilerParams(vmem_limit_bytes=48 << 20),
        cost_estimate=pl.CostEstimate(
            flops=5_500_000_000, bytes_accessed=24 << 20, transcendentals=4096
        ),
        name="classify",
    )(starts, place, table, *weights)
    return scores.T


def trade(value, axis, first):
    pairs = []
    for i in range(4):
        for core in range(2):
            pairs.append((2 * i + core, 2 * (i ^ (1 if first == (core == 0) else 3)) + core))
    return lax.ppermute(value, (axis, "core"), pairs)


def chosen(me, other, core):
    apart = me ^ other
    return jnp.where(apart == 2, 3, jnp.where(apart == 0, 0, jnp.where((apart == 1) == (core == 0), 1, 2)))


def body(
    volume, partner, offsets, starts, classifier, stem_weight, expand_weight, shrink_weight, head_weight
):
    lines, posts = lax.axis_size("line"), lax.axis_size("post")
    line_me, post_me = lax.axis_index("line"), lax.axis_index("post")
    slab_axes = ("column", "core")
    slabs, slab_me = lax.axis_size(slab_axes), lax.axis_index(slab_axes)
    tile_me, core_me = line_me * posts + post_me, lax.axis_index("core")
    own = volume[0]
    planes, rows, width = own.shape

    first, second = pack_parts(
        jnp.reshape(core_me, (1,)).astype(jnp.int32),
        stem_weight[0], expand_weight[0, 0], shrink_weight[0, 0], head_weight[0].T, own,
    )

    def near(value, axis):
        return [value, trade(value, axis, True), trade(value, axis, False)]

    def far(values, axis):
        return values + [trade(values[1], axis, False)]

    stream_a, stream_b = near(first, "post"), near(second, "line")
    own, _ = lax.optimization_barrier((own, first))
    stream_a, stream_b = far(stream_a, "post"), far(stream_b, "line")

    routes = classifier[:, 0]
    places = []
    for core in (core_me, 1 - core_me):
        by_line = chosen(line_me, routes // posts, core)
        by_post = chosen(post_me, routes % posts, core)
        places += [by_line, by_post, by_post, by_line]
    place = jnp.stack(places + [jnp.broadcast_to(core_me, routes.shape)]).astype(jnp.int32)
    scalars = jnp.stack([offsets[tile_me], slab_me, jnp.int32(slabs)])

    up = [(i, i + 1) for i in range(slabs - 1)]
    down = [(j, i) for i, j in up]
    before = lax.ppermute(own[planes - HALO :], slab_axes, up)
    after = lax.ppermute(own[:HALO], slab_axes, down)

    met = jnp.stack([value[:, PART_ROWS:] for value in stream_a])
    sent = []
    for line in range(lines):
        back = chosen(post_me, partner[line * posts + post_me] % posts, core_me)
        sent.append(lax.dynamic_index_in_dim(met, back, 0, keepdims=False))
    sent = jnp.stack(sent)
    all_a = jnp.stack([value[:, :PART_ROWS] for value in stream_a])
    all_b = jnp.stack(stream_b)
    all_a, place, scalars = lax.optimization_barrier((all_a, place, scalars))
    stream_a, stream_b = near(all_a, "line"), near(all_b, "post")
    mates = lax.all_to_all(sent, "line", split_axis=0, concat_axis=0, tiled=True)
    mate = lax.dynamic_index_in_dim(mates, partner[tile_me] // posts, 0, keepdims=False)
    mate = mate.reshape(HALO, rows, 128)
    (stream_a[1], stream_b[1]), mate = lax.optimization_barrier(
        ((stream_a[1], stream_b[1]), mate)
    )
    stream_a, stream_b = far(stream_a, "line"), far(stream_b, "post")

    mate_before = lax.ppermute(mate, slab_axes, up)
    mate_after = lax.ppermute(mate, slab_axes, down)
    log_response, table = filter_band(
        scalars, before, own, after, mate_before, mate, mate_after
    )
    table = table.reshape(width, -1, 128)
    ends, table = lax.optimization_barrier(((stream_a[-1], stream_b[-1]), table))
    stream_a[-1], stream_b[-1] = ends

    swap = [(0, 1), (1, 0)]
    weights = stream_a + stream_b
    weights = weights + [lax.ppermute(value, "core", swap) for value in weights]

    logits = classify(starts, place, table, weights)
    return (log_response[None], logits)


def solution(mesh):
    tiles, slabs = mesh.devices.shape
    split = jax.sharding.Mesh(
        mesh.devices.reshape(4, tiles // 4, slabs // 2, 2), ("line", "post", "column", "core")
    )
    tile, slab = ("line", "post"), ("column", "core")
    both = tile + slab
    return jax.shard_map(
        body,
        mesh=split,
        in_specs=(
            P(tile, slab, None, None),
            P(),
            P(),
            P(both),
            P(both, None),
            P(tile, None, None),
            P(tile, None, None, None),
            P(tile, None, None, None),
            P(tile, None, None),
        ),
        out_specs=(P(tile, slab, None, None), P(both, None)),
        check_vma=False,
    )
```

```python
import functools
import math

import jax
import jax.numpy as jnp
from jax import lax
from jax.experimental import pallas as pl
from jax.experimental.pallas import tpu as pltpu
from jax.sharding import PartitionSpec as P

OV = 32
CX = 64
RADIUS = 3
TOGETHER = 4
HALO = 4
F32 = jnp.float32
BF16 = jnp.bfloat16
HIGH = lax.Precision.HIGHEST

STEM_ROWS, EXPAND_ROWS, SHRINK_ROWS, HEAD_ROWS = 128, 256, 256, 16
EXPAND_AT = STEM_ROWS
SHRINK_AT = EXPAND_AT + EXPAND_ROWS
HEAD_AT = SHRINK_AT + SHRINK_ROWS
PART_ROWS = HEAD_AT + HEAD_ROWS
STRIP_ROWS = 128


def gauss_taps():
    weights_raw = [math.exp(-0.5 * j * j) for j in range(-RADIUS, RADIUS + 1)]
    summed = sum(weights_raw)
    return [value / summed for value in weights_raw]


def pack_kernel(core_ref, stem_ref, expand_ref, shrink_ref, head_ref, own_ref, *refs):
    out_refs, wide_ref = refs[:2], refs[2]
    head = jnp.concatenate(
        [head_ref[:, :128].astype(F32), head_ref[:, 128:].astype(F32)], axis=0
    ).astype(BF16)
    for half in range(2):
        lanes = pl.ds(128 * half, 128)
        wide_ref[...] = stem_ref[:, lanes].astype(F32)
        for local in range(4):
            out_ref, q = out_refs[local // 2], local % 2
            rows = pl.ds(4 * core_ref[0] + local, 64, stride=8)
            out_ref[q, pl.ds(64 * half, 64), :] = wide_ref[rows, :].astype(BF16)
            out_ref[q, pl.ds(SHRINK_AT + 128 * half, 128), :] = shrink_ref[
                pl.ds(128 * local, 128), lanes
            ]
    for local in range(4):
        out_ref, q = out_refs[local // 2], local % 2
        out_ref[q, pl.ds(EXPAND_AT, 256), :] = expand_ref[:, pl.ds(128 * local, 128)]
        out_ref[q, pl.ds(HEAD_AT, 16), :] = head
    planes, rows = own_ref.shape[0], own_ref.shape[1]
    lane = lax.broadcasted_iota(jnp.int32, (rows, 128), 1)
    for i in range(HALO):
        strip = own_ref[i].astype(F32)
        for quarter in range(1, planes // HALO):
            plane = pltpu.roll(own_ref[HALO * quarter + i].astype(F32), OV * quarter, 1)
            strip = jnp.where(lane >= OV * quarter, plane, strip)
        at = PART_ROWS + rows * (i % 2)
        out_refs[0][i // 2, pl.ds(at, rows), :] = strip.astype(BF16)


def pack_parts(core, stem, expand, shrink, head, own):
    wide = pl.BlockSpec((2, PART_ROWS + STRIP_ROWS, 128), lambda i, c: (0, 0, 0))
    whole = pl.BlockSpec((2, PART_ROWS, 128), lambda i, c: (0, 0, 0))
    return pl.pallas_call(
        pack_kernel,
        out_shape=(
            jax.ShapeDtypeStruct((2, PART_ROWS + STRIP_ROWS, 128), BF16),
            jax.ShapeDtypeStruct((2, PART_ROWS, 128), BF16),
        ),
        grid_spec=pltpu.PrefetchScalarGridSpec(
            num_scalar_prefetch=1,
            grid=(1,),
            in_specs=[
                pl.BlockSpec((512, 256), lambda i, c: (0, 0)),
                pl.BlockSpec((256, 512), lambda i, c: (0, c[0])),
                pl.BlockSpec((512, 256), lambda i, c: (c[0], 0)),
                pl.BlockSpec((8, 256), lambda i, c: (0, 0)),
                pl.BlockSpec(own.shape[:2] + (128,), lambda i, c: (0, 0, 0)),
            ],
            out_specs=(wide, whole),
            scratch_shapes=[pltpu.VMEM((512, 128), F32)],
        ),
        cost_estimate=pl.CostEstimate(flops=0, bytes_accessed=2 << 20, transcendentals=0),
        name="pack_parts",
    )(core, stem, expand, shrink, head, own)


def band_kernel(
    scalars_ref, before_ref, own_ref, after_ref, mate_before_ref, mate_ref, mate_after_ref,
    log_ref, table_ref, joined_ref, rows_ref, smooth_ref, columns_ref,
):
    taps = gauss_taps()
    planes, rows, width = own_ref.shape
    offset, slab, slabs = scalars_ref[0], scalars_ref[1], scalars_ref[2]

    lane = lax.broadcasted_iota(jnp.int32, (rows, 128), 1)
    ramp = 0.25 + 0.5 * (lane.astype(F32) + 0.5) / OV
    quarters = planes // HALO

    def stitch(z, raw, strip, quarter):
        raw = raw.astype(F32)
        mate = strip if quarter == 0 else pltpu.roll(strip, 128 - OV * quarter, 1)
        first = raw[:, :128]
        joined_ref[z, :, :128] = jnp.where(lane < OV, ramp * first + (1.0 - ramp) * mate, first)
        joined_ref[z, :, 128:] = raw[:, 128:]

    def turned(ref, i):
        return pltpu.roll(ref[i].astype(F32), offset, 0)

    for i in range(HALO):
        stitch(i, before_ref[i], turned(mate_before_ref, i), quarters - 1)
        stitch(HALO + planes + i, after_ref[i], turned(mate_after_ref, i), 0)
        strip = turned(mate_ref, i)
        for quarter in range(quarters):
            z = HALO * quarter + i
            stitch(HALO + z, own_ref[z], strip, quarter)

    source = lax.broadcasted_iota(jnp.int32, (width, width), 0)
    target = lax.broadcasted_iota(jnp.int32, (width, width), 1)

    def band_matrix(shift):
        out = jnp.zeros((width, width), F32)
        for j in range(-RADIUS, RADIUS + 1):
            out = jnp.where(source - target == shift + j, taps[j + RADIUS], out)
        return out

    along = band_matrix(0)
    beside = jnp.where(target < width - 1, band_matrix(1), 0.0)
    beside = beside + jnp.where(target > 0, band_matrix(-1), 0.0)

    margin = jnp.zeros((planes + 2, 8, width), F32)
    rows_ref[:, :8, :] = margin
    rows_ref[:, 8 + rows :, :] = margin
    smooth_ref[:, :8, :] = margin
    smooth_ref[:, 8 + rows :, :] = margin

    for p in range(planes + 2):
        mixed = taps[0] * joined_ref[p]
        for j in range(1, 2 * RADIUS + 1):
            mixed = mixed + taps[j] * joined_ref[p + j]
        rows_ref[p, pl.ds(8, rows), :] = mixed
        mixed = taps[0] * rows_ref[p, pl.ds(8 - RADIUS, rows), :]
        for j in range(1, 2 * RADIUS + 1):
            mixed = mixed + taps[j] * rows_ref[p, pl.ds(8 - RADIUS + j, rows), :]
        smooth = jnp.dot(mixed, along, precision=HIGH, preferred_element_type=F32)
        if p == 0:
            smooth = jnp.where(slab > 0, smooth, 0.0)
        elif p == planes + 1:
            smooth = jnp.where(slab < slabs - 1, smooth, 0.0)
        else:
            log_ref[p - 1] = jnp.dot(mixed, beside, precision=HIGH, preferred_element_type=F32)
        smooth_ref[p, pl.ds(8, rows), :] = smooth
    for z in range(planes):
        p = z + 1
        here = smooth_ref[p, pl.ds(8, rows), :]
        near = smooth_ref[p - 1, pl.ds(8, rows), :] + smooth_ref[p + 1, pl.ds(8, rows), :]
        near = near + (smooth_ref[p, pl.ds(7, rows), :] + smooth_ref[p, pl.ds(9, rows), :])
        log_ref[z] = near + log_ref[z] - 6.0 * here

    count = (planes // 4) * (rows // 8)
    for a in range(planes // 4):
        for b in range(rows // 8):
            pieces = [
                smooth_ref[4 * a + dz + 1, pl.ds(8 + 8 * b, 8), :] for dz in range(4)
            ] + [log_ref[4 * a + dz, pl.ds(8 * b, 8), :] for dz in range(4)]
            block = jnp.concatenate(pieces, axis=0)
            block = jnp.concatenate([block, pltpu.roll(block, width - 1, 1)], axis=0)
            columns_ref[pl.ds(a * (rows // 8) + b, width, stride=count), :] = block.T
    table_ref[...] = columns_ref[...].astype(BF16)


def filter_band(scalars, before, own, after, mate_before, mate, mate_after):
    planes, rows, width = own.shape
    count = (planes // 4) * (rows // 8)
    whole3 = lambda i, s: (0, 0, 0)
    return pl.pallas_call(
        band_kernel,
        out_shape=(
            jax.ShapeDtypeStruct((planes, rows, width), F32),
            jax.ShapeDtypeStruct((width * count, 128), BF16),
        ),
        grid_spec=pltpu.PrefetchScalarGridSpec(
            num_scalar_prefetch=1,
            grid=(1,),
            in_specs=[
                pl.BlockSpec((HALO, rows, width), whole3),
                pl.BlockSpec((planes, rows, width), whole3),
                pl.BlockSpec((HALO, rows, width), whole3),
            ]
            + [pl.BlockSpec(mate.shape, whole3)] * 3,
            out_specs=(
                pl.BlockSpec((planes, rows, width), whole3),
                pl.BlockSpec((width * count, 128), lambda i, s: (0, 0)),
            ),
            scratch_shapes=[
                pltpu.VMEM((planes + 2 * HALO, rows, width), F32),
                pltpu.VMEM((planes + 2, rows + 16, width), F32),
                pltpu.VMEM((planes + 2, rows + 16, width), F32),
                pltpu.VMEM((width * count, 128), F32),
            ],
        ),
        compiler_params=pltpu.CompilerParams(vmem_limit_bytes=40 << 20),
        cost_estimate=pl.CostEstimate(
            flops=2_000_000_000, bytes_accessed=6 << 20, transcendentals=0
        ),
        name="filter_band",
    )(scalars, before, own, after, mate_before, mate, mate_after)


def classify_kernel(starts_ref, place_ref, table_ref, *refs):
    weight_refs, (out_ref, held_ref, sem) = refs[:16], refs[16:]
    count = out_ref.shape[1]
    core = place_ref[8, 0]

    def copy(source, k, i, piece):
        holder = core if piece < 2 else 1 - core
        parts = pl.ds(4 * holder + 2 * (piece % 2), 2)
        return pltpu.make_async_copy(
            weight_refs[4 * piece + source].at[k], held_ref.at[i, parts], sem.at[i, piece]
        )

    def start(i, carry):
        for piece in range(2):
            chosen_one = place_ref[2 * piece, i]
            k, other_k = place_ref[2 * piece + 1, i], place_ref[2 * piece + 5, i]
            for source in range(4):

                @pl.when(chosen_one == source)
                def _():
                    copy(source, k, i, piece).start()
                    copy((0, 2, 1, 3)[source], other_k, i, piece + 2).start()

        return carry

    lax.fori_loop(0, 2 * TOGETHER, start, 0)
    each = range(TOGETHER)
    lane = lax.broadcasted_iota(jnp.int32, (8, count), 1)

    def group(g, kept):
        first = TOGETHER * g

        @pl.when(first + 2 * TOGETHER < count)
        def _():
            lax.fori_loop(first + 2 * TOGETHER, first + 3 * TOGETHER, start, 0)

        for k in each:
            for piece in range(4):
                copy(0, 0, first + k, piece).wait()

        def rows_of(k, part, at, rows):
            return held_ref[first + k, part, pl.ds(at, rows), :]

        def joined_lanes(k, parts, at, rows):
            halves = [
                jnp.concatenate([rows_of(k, p, at + h * rows, rows) for p in parts], axis=0)
                for h in range(2)
            ]
            return jnp.concatenate(halves, axis=1)

        hidden = []
        for k in each:
            begin = starts_ref[first + k]
            patches = jnp.concatenate(
                [
                    jnp.concatenate(
                        [table_ref[begin + 8 * c + 2 * j] for j in range(4)], axis=1
                    )
                    for c in range(8)
                ],
                axis=0,
            )
            stem = joined_lanes(k, range(8), 0, 64)
            hidden.append(jnp.dot(patches, stem, preferred_element_type=F32))
        wides = [hidden[k].astype(BF16).astype(F32) for k in each]
        normed = []
        for k in each:
            power = jnp.mean(wides[k] * wides[k], axis=-1, keepdims=True)
            normed.append((wides[k] * lax.rsqrt(power + 1e-05)).astype(BF16))
        ups = []
        for k in each:
            expand = jnp.concatenate([rows_of(k, p, EXPAND_AT, 256) for p in range(8)], axis=1)
            wide = jnp.dot(normed[k], expand, preferred_element_type=F32)
            ups.append([jnp.maximum(wide, 0.0).astype(BF16)])
        total = []
        for k in each:
            shrink = joined_lanes(k, range(8), SHRINK_AT, 128)
            total.append(wides[k] + jnp.dot(jnp.concatenate(ups[k], axis=1), shrink, preferred_element_type=F32))
        for k in each:
            last = total[k].astype(BF16).astype(F32)
            pooled = jnp.sum(last, axis=0, keepdims=True) * (1.0 / last.shape[0])
            head = rows_of(k, 0, HEAD_AT, 16).astype(F32)
            products = head[:8] * pooled[:, :128] + head[8:] * pooled[:, 128:]
            scores = jnp.sum(products, axis=1, keepdims=True)
            kept = jnp.where(lane == first + k, scores, kept)
        return kept

    out_ref[...] = lax.fori_loop(0, count // TOGETHER, group, jnp.zeros((8, count), F32))


def classify(starts, place, table, weights):
    count = starts.shape[0]
    scores = pl.pallas_call(
        classify_kernel,
        out_shape=jax.ShapeDtypeStruct((8, count), F32),
        in_specs=[
            pl.BlockSpec(memory_space=pltpu.SMEM),
            pl.BlockSpec(memory_space=pltpu.SMEM),
            pl.BlockSpec(memory_space=pltpu.VMEM),
        ]
        + [pl.BlockSpec(memory_space=pl.ANY)] * len(weights),
        out_specs=pl.BlockSpec(memory_space=pltpu.VMEM),
        scratch_shapes=[
            pltpu.VMEM((count, 8, PART_ROWS, 128), BF16),
            pltpu.SemaphoreType.DMA((count, 4)),
        ],
        compiler_params=pltpu.CompilerParams(vmem_limit_bytes=48 << 20),
        cost_estimate=pl.CostEstimate(
            flops=5_500_000_000, bytes_accessed=24 << 20, transcendentals=4096
        ),
        name="classify",
    )(starts, place, table, *weights)
    return scores.T


def trade(value, axis, first):
    pairs = []
    for i in range(4):
        for core in range(2):
            pairs.append((2 * i + core, 2 * (i ^ (1 if first == (core == 0) else 3)) + core))
    return lax.ppermute(value, (axis, "core"), pairs)


def chosen(me, other, core):
    apart = me ^ other
    return jnp.where(apart == 2, 3, jnp.where(apart == 0, 0, jnp.where((apart == 1) == (core == 0), 1, 2)))


def body(
    volume, partner, offsets, starts, classifier, stem_weight, expand_weight, shrink_weight, head_weight
):
    lines, posts = lax.axis_size("line"), lax.axis_size("post")
    line_me, post_me = lax.axis_index("line"), lax.axis_index("post")
    slab_axes = ("column", "core")
    slabs, slab_me = lax.axis_size(slab_axes), lax.axis_index(slab_axes)
    tile_me, core_me = line_me * posts + post_me, lax.axis_index("core")
    own = volume[0]
    planes, rows, width = own.shape

    first, second = pack_parts(
        jnp.reshape(core_me, (1,)).astype(jnp.int32),
        stem_weight[0], expand_weight[0, 0], shrink_weight[0, 0], head_weight[0].T, own,
    )

    def near(value, axis):
        return [value, trade(value, axis, True), trade(value, axis, False)]

    def far(values, axis):
        return values + [trade(values[1], axis, False)]

    stream_a, stream_b = near(first, "post"), near(second, "line")
    own, _ = lax.optimization_barrier((own, first))
    stream_a, stream_b = far(stream_a, "post"), far(stream_b, "line")

    routes = classifier[:, 0]
    places = []
    for core in (core_me, 1 - core_me):
        by_line = chosen(line_me, routes // posts, core)
        by_post = chosen(post_me, routes % posts, core)
        places += [by_line, by_post, by_post, by_line]
    place = jnp.stack(places + [jnp.broadcast_to(core_me, routes.shape)]).astype(jnp.int32)
    scalars = jnp.stack([offsets[tile_me], slab_me, jnp.int32(slabs)])

    up = [(i, i + 1) for i in range(slabs - 1)]
    down = [(j, i) for i, j in up]
    before = lax.ppermute(own[planes - HALO :], slab_axes, up)
    after = lax.ppermute(own[:HALO], slab_axes, down)

    met = jnp.stack([value[:, PART_ROWS:] for value in stream_a])
    sent = []
    for line in range(lines):
        back = chosen(post_me, partner[line * posts + post_me] % posts, core_me)
        sent.append(lax.dynamic_index_in_dim(met, back, 0, keepdims=False))
    sent = jnp.stack(sent)
    all_a = jnp.stack([value[:, :PART_ROWS] for value in stream_a])
    all_b = jnp.stack(stream_b)
    all_a, place, scalars = lax.optimization_barrier((all_a, place, scalars))
    stream_a, stream_b = near(all_a, "line"), near(all_b, "post")
    mates = lax.all_to_all(sent, "line", split_axis=0, concat_axis=0, tiled=True)
    mate = lax.dynamic_index_in_dim(mates, partner[tile_me] // posts, 0, keepdims=False)
    mate = mate.reshape(HALO, rows, 128)
    (stream_a[1], stream_b[1]), mate, before, after = lax.optimization_barrier(
        ((stream_a[1], stream_b[1]), mate, before, after)
    )
    stream_a, stream_b = far(stream_a, "line"), far(stream_b, "post")

    mate_before = lax.ppermute(mate, slab_axes, up)
    mate_after = lax.ppermute(mate, slab_axes, down)
    log_response, table = filter_band(
        scalars, before, own, after, mate_before, mate, mate_after
    )
    table = table.reshape(width, -1, 128)
    ends, table = lax.optimization_barrier(((stream_a[-1], stream_b[-1]), table))
    stream_a[-1], stream_b[-1] = ends

    swap = [(0, 1), (1, 0)]
    weights = stream_a + stream_b
    weights = weights + [lax.ppermute(value, "core", swap) for value in weights]

    logits = classify(starts, place, table, weights)
    return (log_response[None], logits)


def solution(mesh):
    tiles, slabs = mesh.devices.shape
    split = jax.sharding.Mesh(
        mesh.devices.reshape(4, tiles // 4, slabs // 2, 2), ("line", "post", "column", "core")
    )
    tile, slab = ("line", "post"), ("column", "core")
    both = tile + slab
    return jax.shard_map(
        body,
        mesh=split,
        in_specs=(
            P(tile, slab, None, None),
            P(),
            P(),
            P(both),
            P(both, None),
            P(tile, None, None),
            P(tile, None, None, None),
            P(tile, None, None, None),
            P(tile, None, None),
        ),
        out_specs=(P(tile, slab, None, None), P(both, None)),
        check_vma=False,
    )
```

```python
import functools
import math

import jax
import jax.numpy as jnp
from jax import lax
from jax.experimental import pallas as pl
from jax.experimental.pallas import tpu as pltpu
from jax.sharding import PartitionSpec as P

OV = 32
CX = 64
RADIUS = 3
TOGETHER = 4
HALO = 4
F32 = jnp.float32
BF16 = jnp.bfloat16
HIGH = lax.Precision.HIGHEST

STEM_ROWS, EXPAND_ROWS, SHRINK_ROWS, HEAD_ROWS = 128, 256, 256, 16
EXPAND_AT = STEM_ROWS
SHRINK_AT = EXPAND_AT + EXPAND_ROWS
HEAD_AT = SHRINK_AT + SHRINK_ROWS
PART_ROWS = HEAD_AT + HEAD_ROWS
STRIP_ROWS = 128


def gauss_taps():
    weights_raw = [math.exp(-0.5 * j * j) for j in range(-RADIUS, RADIUS + 1)]
    summed = sum(weights_raw)
    return [value / summed for value in weights_raw]


def pack_kernel(core_ref, stem_ref, expand_ref, shrink_ref, head_ref, own_ref, *refs):
    out_refs, wide_ref = refs[:2], refs[2]
    head = jnp.concatenate(
        [head_ref[:, :128].astype(F32), head_ref[:, 128:].astype(F32)], axis=0
    ).astype(BF16)
    for half in range(2):
        lanes = pl.ds(128 * half, 128)
        wide_ref[...] = stem_ref[:, lanes].astype(F32)
        for local in range(4):
            out_ref, q = out_refs[local // 2], local % 2
            rows = pl.ds(4 * core_ref[0] + local, 64, stride=8)
            out_ref[q, pl.ds(64 * half, 64), :] = wide_ref[rows, :].astype(BF16)
            out_ref[q, pl.ds(SHRINK_AT + 128 * half, 128), :] = shrink_ref[
                pl.ds(128 * local, 128), lanes
            ]
    for local in range(4):
        out_ref, q = out_refs[local // 2], local % 2
        out_ref[q, pl.ds(EXPAND_AT, 256), :] = expand_ref[:, pl.ds(128 * local, 128)]
        out_ref[q, pl.ds(HEAD_AT, 16), :] = head
    planes, rows = own_ref.shape[0], own_ref.shape[1]
    lane = lax.broadcasted_iota(jnp.int32, (rows, 128), 1)
    for i in range(HALO):
        strip = own_ref[i].astype(F32)
        for quarter in range(1, planes // HALO):
            plane = pltpu.roll(own_ref[HALO * quarter + i].astype(F32), OV * quarter, 1)
            strip = jnp.where(lane >= OV * quarter, plane, strip)
        at = PART_ROWS + rows * (i % 2)
        out_refs[0][i // 2, pl.ds(at, rows), :] = strip.astype(BF16)


def pack_parts(core, stem, expand, shrink, head, own):
    wide = pl.BlockSpec((2, PART_ROWS + STRIP_ROWS, 128), lambda i, c: (0, 0, 0))
    whole = pl.BlockSpec((2, PART_ROWS, 128), lambda i, c: (0, 0, 0))
    return pl.pallas_call(
        pack_kernel,
        out_shape=(
            jax.ShapeDtypeStruct((2, PART_ROWS + STRIP_ROWS, 128), BF16),
            jax.ShapeDtypeStruct((2, PART_ROWS, 128), BF16),
        ),
        grid_spec=pltpu.PrefetchScalarGridSpec(
            num_scalar_prefetch=1,
            grid=(1,),
            in_specs=[
                pl.BlockSpec((512, 256), lambda i, c: (0, 0)),
                pl.BlockSpec((256, 512), lambda i, c: (0, c[0])),
                pl.BlockSpec((512, 256), lambda i, c: (c[0], 0)),
                pl.BlockSpec((8, 256), lambda i, c: (0, 0)),
                pl.BlockSpec(own.shape[:2] + (128,), lambda i, c: (0, 0, 0)),
            ],
            out_specs=(wide, whole),
            scratch_shapes=[pltpu.VMEM((512, 128), F32)],
        ),
        cost_estimate=pl.CostEstimate(flops=0, bytes_accessed=2 << 20, transcendentals=0),
        name="pack_parts",
    )(core, stem, expand, shrink, head, own)


def band_kernel(
    scalars_ref, before_ref, own_ref, after_ref, mate_before_ref, mate_ref, mate_after_ref,
    log_ref, table_ref, joined_ref, rows_ref, smooth_ref, columns_ref,
):
    taps = gauss_taps()
    planes, rows, width = own_ref.shape
    offset, slab, slabs = scalars_ref[0], scalars_ref[1], scalars_ref[2]

    lane = lax.broadcasted_iota(jnp.int32, (rows, 128), 1)
    ramp = 0.25 + 0.5 * (lane.astype(F32) + 0.5) / OV
    quarters = planes // HALO

    def stitch(z, raw, strip, quarter):
        raw = raw.astype(F32)
        mate = strip if quarter == 0 else pltpu.roll(strip, 128 - OV * quarter, 1)
        first = raw[:, :128]
        joined_ref[z, :, :128] = jnp.where(lane < OV, ramp * first + (1.0 - ramp) * mate, first)
        joined_ref[z, :, 128:] = raw[:, 128:]

    def turned(ref, i):
        return pltpu.roll(ref[i].astype(F32), offset, 0)

    for i in range(HALO):
        stitch(i, before_ref[i], turned(mate_before_ref, i), quarters - 1)
        stitch(HALO + planes + i, after_ref[i], turned(mate_after_ref, i), 0)
        strip = turned(mate_ref, i)
        for quarter in range(quarters):
            z = HALO * quarter + i
            stitch(HALO + z, own_ref[z], strip, quarter)

    source = lax.broadcasted_iota(jnp.int32, (width, width), 0)
    target = lax.broadcasted_iota(jnp.int32, (width, width), 1)

    def band_matrix(shift):
        out = jnp.zeros((width, width), F32)
        for j in range(-RADIUS, RADIUS + 1):
            out = jnp.where(source - target == shift + j, taps[j + RADIUS], out)
        return out

    along = band_matrix(0)
    beside = jnp.where(target < width - 1, band_matrix(1), 0.0)
    beside = beside + jnp.where(target > 0, band_matrix(-1), 0.0)

    margin = jnp.zeros((planes + 2, 8, width), F32)
    rows_ref[:, :8, :] = margin
    rows_ref[:, 8 + rows :, :] = margin
    smooth_ref[:, :8, :] = margin
    smooth_ref[:, 8 + rows :, :] = margin

    for p in range(planes + 2):
        mixed = taps[0] * joined_ref[p]
        for j in range(1, 2 * RADIUS + 1):
            mixed = mixed + taps[j] * joined_ref[p + j]
        rows_ref[p, pl.ds(8, rows), :] = mixed
        mixed = taps[0] * rows_ref[p, pl.ds(8 - RADIUS, rows), :]
        for j in range(1, 2 * RADIUS + 1):
            mixed = mixed + taps[j] * rows_ref[p, pl.ds(8 - RADIUS + j, rows), :]
        smooth = jnp.dot(mixed, along, precision=HIGH, preferred_element_type=F32)
        if p == 0:
            smooth = jnp.where(slab > 0, smooth, 0.0)
        elif p == planes + 1:
            smooth = jnp.where(slab < slabs - 1, smooth, 0.0)
        else:
            log_ref[p - 1] = jnp.dot(mixed, beside, precision=HIGH, preferred_element_type=F32)
        smooth_ref[p, pl.ds(8, rows), :] = smooth
    for z in range(planes):
        p = z + 1
        here = smooth_ref[p, pl.ds(8, rows), :]
        near = smooth_ref[p - 1, pl.ds(8, rows), :] + smooth_ref[p + 1, pl.ds(8, rows), :]
        near = near + (smooth_ref[p, pl.ds(7, rows), :] + smooth_ref[p, pl.ds(9, rows), :])
        log_ref[z] = near + log_ref[z] - 6.0 * here

    count = (planes // 4) * (rows // 8)
    for a in range(planes // 4):
        for b in range(rows // 8):
            pieces = [
                smooth_ref[4 * a + dz + 1, pl.ds(8 + 8 * b, 8), :] for dz in range(4)
            ] + [log_ref[4 * a + dz, pl.ds(8 * b, 8), :] for dz in range(4)]
            block = jnp.concatenate(pieces, axis=0)
            block = jnp.concatenate([block, pltpu.roll(block, width - 1, 1)], axis=0)
            columns_ref[pl.ds(a * (rows // 8) + b, width, stride=count), :] = block.T
    table_ref[...] = columns_ref[...].astype(BF16)


def filter_band(scalars, before, own, after, mate_before, mate, mate_after):
    planes, rows, width = own.shape
    count = (planes // 4) * (rows // 8)
    whole3 = lambda i, s: (0, 0, 0)
    return pl.pallas_call(
        band_kernel,
        out_shape=(
            jax.ShapeDtypeStruct((planes, rows, width), F32),
            jax.ShapeDtypeStruct((width * count, 128), BF16),
        ),
        grid_spec=pltpu.PrefetchScalarGridSpec(
            num_scalar_prefetch=1,
            grid=(1,),
            in_specs=[
                pl.BlockSpec((HALO, rows, width), whole3),
                pl.BlockSpec((planes, rows, width), whole3),
                pl.BlockSpec((HALO, rows, width), whole3),
            ]
            + [pl.BlockSpec(mate.shape, whole3)] * 3,
            out_specs=(
                pl.BlockSpec((planes, rows, width), whole3),
                pl.BlockSpec((width * count, 128), lambda i, s: (0, 0)),
            ),
            scratch_shapes=[
                pltpu.VMEM((planes + 2 * HALO, rows, width), F32),
                pltpu.VMEM((planes + 2, rows + 16, width), F32),
                pltpu.VMEM((planes + 2, rows + 16, width), F32),
                pltpu.VMEM((width * count, 128), F32),
            ],
        ),
        compiler_params=pltpu.CompilerParams(vmem_limit_bytes=40 << 20),
        cost_estimate=pl.CostEstimate(
            flops=2_000_000_000, bytes_accessed=6 << 20, transcendentals=0
        ),
        name="filter_band",
    )(scalars, before, own, after, mate_before, mate, mate_after)


def classify_kernel(starts_ref, place_ref, table_ref, *refs):
    weight_refs, (out_ref, held_ref, sem) = refs[:16], refs[16:]
    count = out_ref.shape[1]
    core = place_ref[8, 0]

    def copy(source, k, i, piece):
        holder = core if piece < 2 else 1 - core
        parts = pl.ds(4 * holder + 2 * (piece % 2), 2)
        return pltpu.make_async_copy(
            weight_refs[4 * piece + source].at[k], held_ref.at[i, parts], sem.at[i, piece]
        )

    def start(i, carry):
        for piece in range(2):
            chosen_one = place_ref[2 * piece, i]
            k, other_k = place_ref[2 * piece + 1, i], place_ref[2 * piece + 5, i]
            for source in range(4):

                @pl.when(chosen_one == source)
                def _():
                    copy(source, k, i, piece).start()
                    copy((0, 2, 1, 3)[source], other_k, i, piece + 2).start()

        return carry

    lax.fori_loop(0, 2 * TOGETHER, start, 0)
    each = range(TOGETHER)
    lane = lax.broadcasted_iota(jnp.int32, (8, count), 1)

    def group(g, kept):
        first = TOGETHER * g

        @pl.when(first + 2 * TOGETHER < count)
        def _():
            lax.fori_loop(first + 2 * TOGETHER, first + 3 * TOGETHER, start, 0)

        for k in each:
            for piece in range(4):
                copy(0, 0, first + k, piece).wait()

        def rows_of(k, part, at, rows):
            return held_ref[first + k, part, pl.ds(at, rows), :]

        def joined_lanes(k, parts, at, rows):
            halves = [
                jnp.concatenate([rows_of(k, p, at + h * rows, rows) for p in parts], axis=0)
                for h in range(2)
            ]
            return jnp.concatenate(halves, axis=1)

        hidden = []
        for k in each:
            begin = starts_ref[first + k]
            patches = jnp.concatenate(
                [
                    jnp.concatenate(
                        [table_ref[begin + 8 * c + 2 * j] for j in range(4)], axis=1
                    )
                    for c in range(8)
                ],
                axis=0,
            )
            stem = joined_lanes(k, range(8), 0, 64)
            hidden.append(jnp.dot(patches, stem, preferred_element_type=F32))
        wides = [hidden[k].astype(BF16).astype(F32) for k in each]
        normed = []
        for k in each:
            power = jnp.mean(wides[k] * wides[k], axis=-1, keepdims=True)
            normed.append((wides[k] * lax.rsqrt(power + 1e-05)).astype(BF16))
        ups = []
        for k in each:
            expand = jnp.concatenate([rows_of(k, p, EXPAND_AT, 256) for p in range(8)], axis=1)
            wide = jnp.dot(normed[k], expand, preferred_element_type=F32)
            ups.append([jnp.maximum(wide, 0.0).astype(BF16)])
        total = []
        for k in each:
            shrink = joined_lanes(k, range(8), SHRINK_AT, 128)
            total.append(wides[k] + jnp.dot(jnp.concatenate(ups[k], axis=1), shrink, preferred_element_type=F32))
        for k in each:
            last = total[k].astype(BF16).astype(F32)
            pooled = jnp.sum(last, axis=0, keepdims=True) * (1.0 / last.shape[0])
            head = rows_of(k, 0, HEAD_AT, 16).astype(F32)
            products = head[:8] * pooled[:, :128] + head[8:] * pooled[:, 128:]
            scores = jnp.sum(products, axis=1, keepdims=True)
            kept = jnp.where(lane == first + k, scores, kept)
        return kept

    out_ref[...] = lax.fori_loop(0, count // TOGETHER, group, jnp.zeros((8, count), F32))


def classify(starts, place, table, weights):
    count = starts.shape[0]
    scores = pl.pallas_call(
        classify_kernel,
        out_shape=jax.ShapeDtypeStruct((8, count), F32),
        in_specs=[
            pl.BlockSpec(memory_space=pltpu.SMEM),
            pl.BlockSpec(memory_space=pltpu.SMEM),
            pl.BlockSpec(memory_space=pltpu.VMEM),
        ]
        + [pl.BlockSpec(memory_space=pl.ANY)] * len(weights),
        out_specs=pl.BlockSpec(memory_space=pltpu.VMEM),
        scratch_shapes=[
            pltpu.VMEM((count, 8, PART_ROWS, 128), BF16),
            pltpu.SemaphoreType.DMA((count, 4)),
        ],
        compiler_params=pltpu.CompilerParams(vmem_limit_bytes=48 << 20),
        cost_estimate=pl.CostEstimate(
            flops=5_500_000_000, bytes_accessed=24 << 20, transcendentals=4096
        ),
        name="classify",
    )(starts, place, table, *weights)
    return scores.T


def trade(value, axis, first):
    pairs = []
    for i in range(4):
        for core in range(2):
            pairs.append((2 * i + core, 2 * (i ^ (1 if first == (core == 0) else 3)) + core))
    return lax.ppermute(value, (axis, "core"), pairs)


def chosen(me, other, core):
    apart = me ^ other
    return jnp.where(apart == 2, 3, jnp.where(apart == 0, 0, jnp.where((apart == 1) == (core == 0), 1, 2)))


def body(
    volume, partner, offsets, starts, classifier, stem_weight, expand_weight, shrink_weight, head_weight
):
    lines, posts = lax.axis_size("line"), lax.axis_size("post")
    line_me, post_me = lax.axis_index("line"), lax.axis_index("post")
    slab_axes = ("column", "core")
    slabs, slab_me = lax.axis_size(slab_axes), lax.axis_index(slab_axes)
    tile_me, core_me = line_me * posts + post_me, lax.axis_index("core")
    own = volume[0]
    planes, rows, width = own.shape

    first, second = pack_parts(
        jnp.reshape(core_me, (1,)).astype(jnp.int32),
        stem_weight[0], expand_weight[0, 0], shrink_weight[0, 0], head_weight[0].T, own,
    )

    def near(value, axis):
        second_trade = trade(value, axis, False)
        return [value, trade(value, axis, True), second_trade]

    def far(values, axis):
        return values + [trade(values[1], axis, False)]

    stream_a, stream_b = near(first, "post"), near(second, "line")
    own, _ = lax.optimization_barrier((own, first))
    stream_a, stream_b = far(stream_a, "post"), far(stream_b, "line")

    routes = classifier[:, 0]
    places = []
    for core in (core_me, 1 - core_me):
        by_line = chosen(line_me, routes // posts, core)
        by_post = chosen(post_me, routes % posts, core)
        places += [by_line, by_post, by_post, by_line]
    place = jnp.stack(places + [jnp.broadcast_to(core_me, routes.shape)]).astype(jnp.int32)
    scalars = jnp.stack([offsets[tile_me], slab_me, jnp.int32(slabs)])

    up = [(i, i + 1) for i in range(slabs - 1)]
    down = [(j, i) for i, j in up]
    before = lax.ppermute(own[planes - HALO :], slab_axes, up)
    after = lax.ppermute(own[:HALO], slab_axes, down)

    met = jnp.stack([value[:, PART_ROWS:] for value in stream_a])
    sent = []
    for line in range(lines):
        back = chosen(post_me, partner[line * posts + post_me] % posts, core_me)
        sent.append(lax.dynamic_index_in_dim(met, back, 0, keepdims=False))
    sent = jnp.stack(sent)
    all_a = jnp.stack([value[:, :PART_ROWS] for value in stream_a])
    all_b = jnp.stack(stream_b)
    all_a, place, scalars = lax.optimization_barrier((all_a, place, scalars))
    stream_a, stream_b = near(all_a, "line"), near(all_b, "post")
    mates = lax.all_to_all(sent, "line", split_axis=0, concat_axis=0, tiled=True)
    mate = lax.dynamic_index_in_dim(mates, partner[tile_me] // posts, 0, keepdims=False)
    mate = mate.reshape(HALO, rows, 128)
    (stream_a[1], stream_b[1]), mate, before, after = lax.optimization_barrier(
        ((stream_a[1], stream_b[1]), mate, before, after)
    )
    stream_a, stream_b = far(stream_a, "line"), far(stream_b, "post")

    mate_before = lax.ppermute(mate, slab_axes, up)
    mate_after = lax.ppermute(mate, slab_axes, down)
    log_response, table = filter_band(
        scalars, before, own, after, mate_before, mate, mate_after
    )
    table = table.reshape(width, -1, 128)
    ends, table = lax.optimization_barrier(((stream_a[-1], stream_b[-1]), table))
    stream_a[-1], stream_b[-1] = ends

    swap = [(0, 1), (1, 0)]
    weights = stream_a + stream_b
    weights = weights + [lax.ppermute(value, "core", swap) for value in weights]

    logits = classify(starts, place, table, weights)
    return (log_response[None], logits)


def solution(mesh):
    tiles, slabs = mesh.devices.shape
    split = jax.sharding.Mesh(
        mesh.devices.reshape(4, tiles // 4, slabs // 2, 2), ("line", "post", "column", "core")
    )
    tile, slab = ("line", "post"), ("column", "core")
    both = tile + slab
    return jax.shard_map(
        body,
        mesh=split,
        in_specs=(
            P(tile, slab, None, None),
            P(),
            P(),
            P(both),
            P(both, None),
            P(tile, None, None),
            P(tile, None, None, None),
            P(tile, None, None, None),
            P(tile, None, None),
        ),
        out_specs=(P(tile, slab, None, None), P(both, None)),
        check_vma=False,
    )
```
